32 devices in a mesh: ctx: 16 (over z, y, x), ch: 2 (over core).
Axes of the slice: x: 2, y: 2, z: 4, core: 2. Of those that a mesh axis runs over, the one named last changes fastest.
Arguments:
- signal: bfloat16 [4096, 512], P('ctx', 'ch'), may hold values from -6 to 6
- gating: bfloat16 [4096, 512], P('ctx', 'ch'), may hold values from -6 to 6
- filter_taps: bfloat16 [4096], P('ctx'), may hold values from -4 to 4
- cotangent: bfloat16 [4096, 512], P('ctx', 'ch'), may hold values from -6 to 6
Outputs:
- grad_signal: bfloat16 [4096, 512], P('ctx', 'ch')
- grad_gating: bfloat16 [4096, 512], P('ctx', 'ch')
- grad_taps: float32 [4096], P('ctx')
The draws below stay inside these ranges and needn't reach their ends.
All inputs are finite; a program needn't handle non-finite values.
Results may differ from the reference program's by a relative error of at most 0.0069.
Values may be sent and summed in bfloat16 or wider, within the bound.
A program may use at most 64 MiB of HBM per device.

```python
import math
import jax
import jax.numpy as jnp
from jax import lax

CHANNELS = 512
BLOCK = 256
BLOCKS = 16
SEQUENCE_LENGTH = 4096


def draw_filter_taps(key, part):
    subkeys = jax.random.split(key, 5)
    step_floats = jnp.arange(SEQUENCE_LENGTH, dtype=jnp.int32).astype(jnp.float32)
    random_jitter = jnp.clip(jax.random.normal(subkeys[0], (SEQUENCE_LENGTH,), jnp.float32), -4.0, 4.0)
    fast_scale = jax.random.uniform(subkeys[1], (), jnp.float32, 0.2, 0.3) * BLOCK
    slow_scale = jax.random.uniform(subkeys[2], (), jnp.float32, 0.5, 2.0) * SEQUENCE_LENGTH
    split_positions = jax.random.randint(subkeys[3], (3,), 0, SEQUENCE_LENGTH)
    decline_amounts = jax.random.uniform(subkeys[4], (3,), jnp.float32, 0.5, 0.8)
    fast_share = 0.3
    fast_amp = jnp.sqrt(2.0 * fast_share / fast_scale)
    slow_total = (1.0 - jnp.exp(-2.0 * SEQUENCE_LENGTH / slow_scale)) / (1.0 - jnp.exp(-2.0 / slow_scale))
    slow_amp = jnp.sqrt((1.0 - fast_share) / slow_total)
    slow_amplitude_curve = slow_amp * jnp.exp(-step_floats / slow_scale)
    amplitude_curve = fast_amp * jnp.exp(-step_floats / fast_scale) + slow_amplitude_curve
    spike_events = jnp.ones((SEQUENCE_LENGTH,), jnp.float32)
    for selected_choice in range(3):
        spike_events = spike_events * jnp.where(step_floats >= split_positions[selected_choice].astype(jnp.float32), decline_amounts[selected_choice], 1.0)
    filter_coefficients = random_jitter * amplitude_curve * spike_events
    return filter_coefficients.astype(jnp.bfloat16)


def level_of(stream_key, dims, cuts, low, largest):
    factor_of = 1.0
    for position, parts in cuts:
        steps = jax.random.uniform(jax.random.fold_in(jax.random.fold_in(stream_key, 6), position), (parts,), jnp.float32, low / len(cuts), largest / len(cuts))
        factor_of = factor_of * jnp.repeat(jnp.exp(steps), dims[position] // parts).reshape((-1,) + (1,) * (len(dims) - 1 - position))
    return factor_of


def gaussian(own_key, extent, scale, reach, pieces=(), held_as=jnp.bfloat16):
    values = scale * jax.random.normal(own_key, extent, jnp.float32)
    if pieces:
        values = values * level_of(own_key, extent, pieces, -0.22, 0.18)
    return jnp.clip(values, -reach, reach).astype(held_as)


def setup_inputs(seed: int = 0) -> dict:
    key_of = jax.random.split(jax.random.key(seed), 5)
    signal = gaussian(key_of[0], (SEQUENCE_LENGTH, CHANNELS), 1.0, 6.0, ((0, 16), (1, 2)))
    gating = gaussian(key_of[1], (SEQUENCE_LENGTH, CHANNELS), 1.0, 6.0, ((0, 16), (1, 2)))
    filter_taps = draw_filter_taps(jax.random.fold_in(key_of[4], 71), 0)
    cotangent = gaussian(key_of[3], (SEQUENCE_LENGTH, CHANNELS), 1.0, 6.0, ((0, 16), (1, 2)))
    return dict(signal=signal, gating=gating, filter_taps=filter_taps, cotangent=cotangent)


highest = lax.Precision.HIGHEST

def build_tables(block_len):
    positions = jnp.arange(block_len, dtype=jnp.int32)
    period_len = 2 * block_len
    early_phase = positions[:, None] * positions[None, :] % period_len
    late_phase = (positions[:, None] + block_len) * positions[None, :] % period_len
    early_angle = early_phase.astype(jnp.float32) * (math.pi / block_len)
    late_angle = late_phase.astype(jnp.float32) * (math.pi / block_len)
    weight = jnp.where(positions == 0, 1.0, 2.0).astype(jnp.float32)
    sign_row = jnp.where(positions % 2 == 0, 1.0, -1.0).astype(jnp.float32)
    forward_cos = jnp.cos(early_angle).astype(jnp.bfloat16)
    forward_sin = (-jnp.sin(early_angle)).astype(jnp.bfloat16)
    early_cos = weight[None, :] * jnp.cos(early_angle)
    early_sin = -weight[None, :] * jnp.sin(early_angle)
    late_cos = weight[None, :] * jnp.cos(late_angle)
    late_sin = -weight[None, :] * jnp.sin(late_angle)
    return (forward_cos, forward_sin, early_cos, early_sin, late_cos, late_sin, sign_row)

def rounded(values):
    return lax.optimization_barrier(values.astype(jnp.bfloat16)).astype(jnp.float32)

def column_spectra(blocks, tables):
    forward_cos = tables[0].astype(jnp.float32)
    forward_sin = tables[1].astype(jnp.float32)
    values = blocks.astype(jnp.float32)
    real_part = jnp.einsum('fn,knc->kfc', forward_cos, values, precision=highest)
    imag_part = jnp.einsum('fn,knc->kfc', forward_sin, values, precision=highest)
    nyquist = jnp.einsum('n,knc->kc', tables[6], values, precision=highest)[:, None, :]
    return (real_part, imag_part, nyquist)

def earlier_blocks(member):
    return jnp.concatenate([jnp.zeros_like(member[:1]), member[:-1]], axis=0)

def pair_sums(v_spec, d_spec, f_spec, block_count):
    low_pad = tuple((jnp.concatenate([jnp.zeros_like(member), member], axis=0) for member in v_spec))
    high_pad = tuple((jnp.concatenate([member, jnp.zeros_like(member)], axis=0) for member in d_spec))

    def accumulate(running, offset):
        f_re, f_im, f_nyq = (lax.dynamic_slice_in_dim(member, offset, 1, 0) for member in f_spec)
        v_re, v_im, v_nyq = (lax.dynamic_slice_in_dim(member, block_count - offset, block_count, 0) for member in low_pad)
        d_re, d_im, d_nyq = (lax.dynamic_slice_in_dim(member, offset, block_count, 0) for member in high_pad)
        updated = (running[0] + f_re * v_re - f_im * v_im, running[1] + f_re * v_im + f_im * v_re, running[2] + f_nyq * v_nyq, running[3] + f_re * d_re + f_im * d_im, running[4] + f_re * d_im - f_im * d_re, running[5] + f_nyq * d_nyq)
        return (updated, None)
    initial = tuple((jnp.zeros_like(member) for member in v_spec + v_spec))
    totals, unused = lax.scan(accumulate, initial, jnp.arange(block_count, dtype=jnp.int32))
    return totals

def lag_sums(v_spec, d_spec, block_count, block_len):
    high_pad = tuple((jnp.concatenate([member, jnp.zeros_like(member)], axis=0) for member in d_spec))

    def accumulate(running, anchor):
        d_re, d_im, d_nyq = (lax.dynamic_slice_in_dim(member, anchor, block_count, 0) for member in high_pad)
        v_re, v_im, v_nyq = (lax.dynamic_slice_in_dim(member, anchor, 1, 0) for member in v_spec)
        updated = (running[0] + lax.optimization_barrier(jnp.sum(d_re * v_re + d_im * v_im, axis=2)), running[1] + lax.optimization_barrier(jnp.sum(d_im * v_re - d_re * v_im, axis=2)), running[2] + lax.optimization_barrier(jnp.sum(d_nyq * v_nyq, axis=2)))
        return (updated, None)
    initial = (jnp.zeros((block_count, block_len), jnp.float32), jnp.zeros((block_count, block_len), jnp.float32), jnp.zeros((block_count, 1), jnp.float32))
    totals, unused = lax.scan(accumulate, initial, jnp.arange(block_count, dtype=jnp.int32))
    return totals

def inverse_signal(real_part, imag_part, nyquist, cos_table, sin_table, sign_row, block_len):
    output = jnp.einsum('tf,kfc->ktc', rounded(cos_table), rounded(real_part), precision=highest)
    output = output + jnp.einsum('tf,kfc->ktc', rounded(sin_table), rounded(imag_part), precision=highest)
    return (output + sign_row[None, :, None] * nyquist) / (2.0 * block_len)

def inverse_taps(real_part, imag_part, nyquist, cos_table, sin_table, sign_row, block_len):
    output = jnp.einsum('tf,kf->kt', cos_table, real_part, precision=highest)
    output = output + jnp.einsum('tf,kf->kt', sin_table, imag_part, precision=highest)
    return (output + sign_row[None, :] * nyquist) / (2.0 * block_len)

def reference(signal, gating, filter_taps, cotangent):
    tables = build_tables(BLOCK)
    sign_row = tables[6]
    flip_col = sign_row[None, :, None]
    grad_mid = (cotangent.astype(jnp.float32) * gating.astype(jnp.float32)).astype(jnp.bfloat16)
    v_spec = column_spectra(signal.reshape(BLOCKS, BLOCK, CHANNELS), tables)
    d_raw = column_spectra(grad_mid.reshape(BLOCKS, BLOCK, CHANNELS), tables)
    d_spec = (d_raw[0] * flip_col, d_raw[1] * flip_col, d_raw[2])
    g_spec = column_spectra(filter_taps.reshape(BLOCKS, BLOCK, 1), tables)
    f_spec = (earlier_blocks(g_spec[0]) + flip_col * g_spec[0], earlier_blocks(g_spec[1]) + flip_col * g_spec[1], earlier_blocks(g_spec[2]) + g_spec[2])
    totals = pair_sums(v_spec, d_spec, f_spec, BLOCKS)
    recomputed = inverse_signal(totals[0], totals[1], totals[2], tables[4], tables[5], sign_row, BLOCK)
    recomputed = recomputed.reshape(SEQUENCE_LENGTH, CHANNELS)
    grad_gating = (cotangent.astype(jnp.float32) * recomputed).astype(jnp.bfloat16)
    grad_signal = inverse_signal(totals[3], totals[4], totals[5], tables[2], tables[3], sign_row, BLOCK)
    grad_signal = grad_signal.reshape(SEQUENCE_LENGTH, CHANNELS).astype(jnp.bfloat16)
    lag_re, lag_im, lag_nyq = lag_sums(v_spec, d_spec, BLOCKS, BLOCK)
    upper_half = inverse_taps(lag_re, lag_im, lag_nyq, tables[4], tables[5], sign_row, BLOCK)
    lower_half = inverse_taps(lag_re, lag_im, lag_nyq, tables[2], tables[3], sign_row, BLOCK)
    following = jnp.concatenate([lower_half[1:], jnp.zeros_like(lower_half[:1])], axis=0)
    grad_taps = ((upper_half + following) / math.sqrt(CHANNELS * SEQUENCE_LENGTH)).reshape(SEQUENCE_LENGTH)
    return (grad_signal, grad_gating, grad_taps)
```

```python
import functools
import math

import jax
import jax.numpy as jnp
from jax import lax
from jax.experimental import pallas as pl
from jax.experimental.pallas import tpu as pltpu
from jax.sharding import PartitionSpec as P

WORKERS = 8
f32 = jnp.float32
bf16 = jnp.bfloat16
NT = (((1,), (1,)), ((), ()))
TN = (((0,), (0,)), ((), ()))


def kernel(
    n, workers, first, norm,
    signal_hbm, gating_hbm, taps_hbm, cot_hbm,
    gs_ref, gg_ref, gt_ref,
    signal_ref, gating_ref, taps_ref, cot_ref, flip,
    tsend, gsend, vsend, taps_all, gpad, vpad,
    ysend, bsend, lsend, yret, bret, lret,
    hpad, toep, acc, mlag,
    s_t, s_g, s_v, s_y0, s_y, s_b, s_l, s_lo,
    r_t, r_g, r_v, r_y, r_b, r_l, s_in, mate_in,
):
    block, width = signal_ref.shape
    half = block // 2
    rows = width // workers
    total = n * rows
    unrolled = n <= 16
    me = lax.axis_index("ctx")
    ch = lax.axis_index("ch")
    mate = 1 - ch
    pieces = lax.axis_size("ch")
    slot = me - first
    is_worker = jnp.logical_and(me >= first, me < first + workers)

    barrier = pltpu.get_barrier_semaphore()

    @pl.when(is_worker)
    def _():
        def greet(d, _):
            pl.semaphore_signal(barrier, inc=1, device_id={"ctx": lax.rem(me + d, n)})
            return 0

        lax.fori_loop(1, n, greet, 0)
        if pieces == 2:
            pl.semaphore_signal(barrier, inc=1, device_id={"ch": mate})

    fetches = [
        pltpu.make_async_copy(src, dst, s_in.at[i])
        for i, (src, dst) in enumerate(
            ((taps_hbm, taps_ref), (cot_hbm, cot_ref), (gating_hbm, gating_ref), (signal_hbm, signal_ref))
        )
    ]
    for fetch in fetches:
        fetch.start()

    def remote(src, dst, send, recv, where):
        return pltpu.make_async_remote_copy(src_ref=src, dst_ref=dst, send_sem=send, recv_sem=recv, device_id=where)

    def drain(ref, sem):
        pltpu.make_async_copy(ref, ref, sem).wait()

    own_step = (-first) % workers

    def to_workers(src, dst, send, recv):
        for i in range(workers):
            p = lax.rem(me + i, workers)
            copy = remote(src(p), dst.at[me], send, recv, {"ctx": first + p})
            if i != own_step:
                copy.start()
            else:
                pl.when(jnp.logical_not(is_worker))(copy.start)

                @pl.when(is_worker)
                def _():
                    pltpu.make_async_copy(src(p), dst.at[me], recv).start()

    across = lax.broadcasted_iota(jnp.int32, (block, block), 0)
    along = lax.broadcasted_iota(jnp.int32, (block, block), 1)
    flip[...] = jnp.where(across + along == block - 1, 1.0, 0.0).astype(bf16)

    fetches[0].wait()
    own_taps = jnp.broadcast_to(taps_ref[...].astype(f32).reshape(1, block), (16, block)).astype(bf16)
    tsend[...] = jnp.dot(own_taps, flip[...], preferred_element_type=f32)[:1]
    fetches[1].wait()
    fetches[2].wait()
    grad_mid = (cot_ref[...].astype(f32) * gating_ref[...].astype(f32)).astype(bf16)
    gsend[...] = grad_mid.astype(f32).T.astype(bf16).reshape(workers, rows, block)
    pl.semaphore_wait(barrier, workers)
    to_workers(lambda p: tsend, taps_all, s_t, r_t)
    to_workers(lambda p: gsend.at[p], gpad, s_g, r_g)
    fetches[3].wait()
    vsend[...] = (
        lax.dot_general(signal_ref[...], flip[...], TN, preferred_element_type=f32)
        .astype(bf16)
        .reshape(workers, rows, block)
    )
    to_workers(lambda p: vsend.at[p], vpad, s_v, r_v)

    def at(k, size):
        return k * size if isinstance(k, int) else pl.multiple_of(k * size, half)

    def table(k):
        start = at(n - k, block)
        upper = toep[:, pl.ds(start, block)]
        lower = toep[:, pl.ds(start - half if isinstance(k, int) else pl.multiple_of(start - half, half), block)]
        return jnp.concatenate([upper, lower], axis=0)

    def over(count, step):
        if unrolled:
            for k in range(count):
                step(k)
        else:
            lax.fori_loop(0, count, lambda k, _: (step(k), 0)[1], 0)

    def backward_step(k):
        if unrolled:
            term = jnp.dot(
                gpad[k:n].reshape(total - k * rows, block), table(k), preferred_element_type=f32
            )
            if k == 0:
                acc[...] = term
            else:
                acc[: total - k * rows] += term
        else:
            acc[:total] += jnp.dot(
                gpad[pl.ds(k, n)].reshape(total, block), table(k), preferred_element_type=f32
            )

    def forward_step(k):
        if unrolled:
            term = jnp.dot(
                vpad[: n - k].reshape(total - k * rows, block), table(k), preferred_element_type=f32
            )
            if k == 0:
                acc[...] = term
            else:
                acc[k * rows :] += term
        else:
            start = pl.multiple_of(k * rows, 16)
            acc[pl.ds(start, total)] += jnp.dot(
                vpad[...].reshape(total, block), table(k), preferred_element_type=f32
            )

    def lag_step(k):
        if unrolled:
            left, right = vpad[: n - k].reshape(total - k * rows, block), gpad[k:n].reshape(total - k * rows, block)
        else:
            left, right = vpad[...].reshape(total, block), gpad[pl.ds(k, n)].reshape(total, block)
        mlag[:, pl.ds(at(k, block), block)] = lax.dot_general(left, right, TN, preferred_element_type=f32)

    def fold(k):
        span = block + half
        start = at(k, block)
        later = start + half if unrolled else pl.multiple_of(start + half, half)
        part = mlag[:half, pl.ds(later, span)] + mlag[half:, pl.ds(start, span)]
        turned = pltpu.roll(part, 1, 1, stride=1, stride_axis=0)[:, half:]
        lsend[pl.ds(k, 1)] = jnp.sum(turned, axis=0, keepdims=True)[None]

    def to_all(src, dst, send, recv, skip):
        def step(d, _):
            q = lax.rem(me + d, n)

            @pl.when(q >= skip)
            def _():
                remote(src.at[q], dst.at[slot], send, recv, {"ctx": q}).start()
            return 0

        lax.fori_loop(1, n, step, 0)

        @pl.when(me >= skip)
        def _():
            pltpu.make_async_copy(src.at[me], dst.at[slot], recv).start()

    @pl.when(is_worker)
    def _():
        if not unrolled:
            gpad[n:] = jnp.zeros((n, rows, block), bf16)
        hpad[...] = jnp.zeros(hpad.shape, f32)
        mlag[:, n * block :] = jnp.zeros((block, block), f32)
        drain(taps_all, r_t)
        for j in range(n):
            start = half + (n - 1 - j) * block
            hpad[:, start : start + block] = taps_all[j]
        for j in range(n + 1):
            window = jnp.broadcast_to(hpad[:, j * block : (j + 1) * block + half], (half, block + half))
            turned = pltpu.roll(window, 1, 1, stride=1, stride_axis=0)
            toep[:, j * block : (j + 1) * block] = turned[:, half:].astype(bf16)
        drain(gpad.at[:n], r_g)
        if pieces == 2:
            pl.semaphore_signal(mate_in, inc=1, device_id={"ch": mate})
        if not unrolled:
            acc[...] = jnp.zeros(acc.shape, f32)
        over(n, backward_step)
        bsend[...] = acc[:total].astype(bf16).reshape(n, rows, block)
        to_all(bsend, bret, s_b, r_b, 0)

        drain(vpad, r_v)
        ysend[0] = jnp.dot(vpad[0], table(0), preferred_element_type=f32).astype(bf16)

        @pl.when(me != 0)
        def _():
            remote(ysend.at[0], yret.at[slot], s_y0, r_y, {"ctx": 0}).start()

        @pl.when(me == 0)
        def _():
            pltpu.make_async_copy(ysend.at[0], yret.at[slot], r_y).start()

        over(n, lag_step)
        over(n, fold)
        if pieces == 2:
            pl.semaphore_wait(mate_in, 1)
        where = ch * workers + slot

        def send_lags(d, _):
            q = d + (d >= me).astype(jnp.int32)
            remote(lsend.at[q], lret.at[where], s_l, r_l, {"ctx": q}).start()
            return 0

        lax.fori_loop(0, n - 1, send_lags, 0)
        pltpu.make_async_copy(lsend.at[me], lret.at[where], r_l).start()
        if pieces == 2:
            def send_other(q, _):
                remote(lsend.at[q], lret.at[where], s_lo, r_l, {"ctx": q, "ch": mate}).start()
                return 0

            lax.fori_loop(0, n, send_other, 0)

        if not unrolled:
            acc[...] = jnp.zeros(acc.shape, f32)
        over(n, forward_step)
        ysend[1:] = acc[rows:total].astype(bf16).reshape(n - 1, rows, block)
        to_all(ysend, yret, s_y, r_y, 1)

    drain(bret, r_b)
    gs_ref[...] = bret[...].reshape(width, block).astype(f32).T.astype(bf16)
    drain(yret, r_y)
    recomputed = lax.dot_general(flip[...], yret[...].reshape(width, block), NT, preferred_element_type=f32)
    gg_ref[...] = (cot_ref[...].astype(f32) * recomputed).astype(bf16)
    drain(lret, r_l)
    gt_ref[...] = jnp.sum(lret[...], axis=0) * norm

    @pl.when(is_worker)
    def _():
        drain(taps_all.at[: workers - 1], s_t)
        drain(gsend.at[: workers - 1], s_g)
        drain(vsend.at[: workers - 1], s_v)
        drain(bsend.at[: n - 1], s_b)
        drain(lsend.at[: n - 1], s_l)
        if pieces == 2:
            drain(lsend, s_lo)

        @pl.when(me != 0)
        def _():
            drain(ysend.at[0], s_y0)
            drain(ysend.at[: n - 2], s_y)

        @pl.when(me == 0)
        def _():
            drain(ysend.at[: n - 1], s_y)

    @pl.when(jnp.logical_not(is_worker))
    def _():
        drain(taps_all.at[:workers], s_t)
        drain(gsend, s_g)
        drain(vsend, s_v)


def store(gs_in, gg_in, gt_in, gs_out, gg_out, gt_out, sems):
    copies = [
        pltpu.make_async_copy(src, dst, sems.at[i])
        for i, (src, dst) in enumerate(((gs_in, gs_out), (gg_in, gg_out), (gt_in, gt_out)))
    ]
    for copy in copies:
        copy.start()
    for copy in copies:
        copy.wait()


def body(signal, gating, filter_taps, cotangent):
    block, width = signal.shape
    n = lax.axis_size("ctx")
    pieces = lax.axis_size("ch")
    workers = min(WORKERS, n)
    first = (n - workers) // 2
    rows = width // workers
    norm = 1.0 / math.sqrt(width * pieces * block * n)
    pad = 0 if n <= 16 else n
    hbm = pl.BlockSpec(memory_space=pltpu.HBM)
    vmem = pl.BlockSpec(memory_space=pltpu.VMEM)
    dma = pltpu.SemaphoreType.DMA
    results = (
        pltpu.VMEM((block, width), bf16),
        pltpu.VMEM((block, width), bf16),
        pltpu.VMEM((1, block), f32),
    )
    outputs = pl.pallas_call(
        functools.partial(kernel, n, workers, first, norm),
        out_shape=results,
        in_specs=[hbm] * 4,
        out_specs=(vmem,) * 3,
        scratch_shapes=[
            pltpu.VMEM((block, width), bf16),
            pltpu.VMEM((block, width), bf16),
            pltpu.VMEM((block,), bf16),
            pltpu.VMEM((block, width), bf16),
            pltpu.VMEM((block, block), bf16),
            pltpu.VMEM((1, block), f32),
            pltpu.VMEM((workers, rows, block), bf16),
            pltpu.VMEM((workers, rows, block), bf16),
            pltpu.VMEM((n, 1, block), f32),
            pltpu.VMEM((n + pad, rows, block), bf16),
            pltpu.VMEM((n, rows, block), bf16),
            pltpu.VMEM((n, rows, block), bf16),
            pltpu.VMEM((n, rows, block), bf16),
            pltpu.VMEM((n, 1, block), f32),
            pltpu.VMEM((workers, rows, block), bf16),
            pltpu.VMEM((workers, rows, block), bf16),
            pltpu.VMEM((pieces * workers, 1, block), f32),
            pltpu.VMEM((1, (n + 1) * block + block // 2), f32),
            pltpu.VMEM((block // 2, (n + 1) * block), bf16),
            pltpu.VMEM(((n + pad) * rows, block), f32),
            pltpu.VMEM((block, (n + 1) * block), f32),
        ]
        + [dma] * 14
        + [dma((4,)), pltpu.SemaphoreType.REGULAR],
        compiler_params=pltpu.CompilerParams(
            collective_id=0, has_side_effects=True, vmem_limit_bytes=60 * 1024 * 1024
        ),
    )(signal, gating, filter_taps, cotangent)
    outputs = [pltpu.with_memory_space_constraint(o, pltpu.VMEM) for o in outputs]
    grad_signal, grad_gating, grad_taps = pl.pallas_call(
        store,
        out_shape=(
            jax.ShapeDtypeStruct((block, width), bf16),
            jax.ShapeDtypeStruct((block, width), bf16),
            jax.ShapeDtypeStruct((1, block), f32),
        ),
        in_specs=[vmem] * 3,
        out_specs=(hbm,) * 3,
        scratch_shapes=[dma((3,))],
    )(*outputs)
    return (grad_signal, grad_gating, grad_taps.reshape(block))


def solution(mesh):
    in_specs = (P("ctx", "ch"), P("ctx", "ch"), P("ctx"), P("ctx", "ch"))
    out_specs = (P("ctx", "ch"), P("ctx", "ch"), P("ctx"))
    return jax.shard_map(body, mesh=mesh, in_specs=in_specs, out_specs=out_specs, check_vma=False)
```

```python
import functools
import math

import jax
import jax.numpy as jnp
from jax import lax
from jax.experimental import pallas as pl
from jax.experimental.pallas import tpu as pltpu
from jax.sharding import PartitionSpec as P

WORKERS = 8
f32 = jnp.float32
bf16 = jnp.bfloat16
NT = (((1,), (1,)), ((), ()))
TN = (((0,), (0,)), ((), ()))


def kernel(
    n, workers, first, norm,
    signal_hbm, gating_hbm, taps_hbm, cot_hbm,
    gs_ref, gg_ref, gt_ref,
    signal_ref, gating_ref, taps_ref, cot_ref, flip,
    tsend, gsend, vsend, taps_all, gpad, vpad,
    ysend, bsend, lsend, yret, bret, lret,
    hpad, toep, acc, mlag,
    s_t, s_g, s_v, s_y0, s_y, s_b, s_l0, s_lo0, s_l, s_lo,
    r_t, r_g, r_v, r_y, r_b, r_l, s_in, mate_in, heard,
):
    block, width = signal_ref.shape
    half = block // 2
    rows = width // workers
    total = n * rows
    unrolled = n <= 16
    me = lax.axis_index("ctx")
    ch = lax.axis_index("ch")
    mate = 1 - ch
    slot = me - first
    is_worker = jnp.logical_and(me >= first, me < first + workers)

    barrier = pltpu.get_barrier_semaphore()

    near = is_worker & (slot < workers // 2)
    far = is_worker & (slot >= workers // 2)

    def greet(core):
        for d in range(1, n):
            pl.semaphore_signal(barrier, inc=1, device_id={"ctx": lax.rem(me + d, n), "ch": core})
        pl.when(ch != core)(lambda: pl.semaphore_signal(barrier, inc=1, device_id={"ch": core}))

    pl.semaphore_signal(barrier, inc=1, device_id={"ch": mate})
    pl.when(near)(lambda: greet(0))
    pl.when(far)(lambda: greet(1))

    fetches = [
        pltpu.make_async_copy(src, dst, s_in.at[i])
        for i, (src, dst) in enumerate(
            ((taps_hbm, taps_ref), (cot_hbm, cot_ref), (gating_hbm, gating_ref), (signal_hbm, signal_ref))
        )
    ]
    for fetch in fetches:
        fetch.start()

    def remote(src, dst, send, recv, where):
        return pltpu.make_async_remote_copy(src_ref=src, dst_ref=dst, send_sem=send, recv_sem=recv, device_id=where)

    def drain(ref, sem):
        pltpu.make_async_copy(ref, ref, sem).wait()

    def to_workers(base, src, dst, send, recv):
        for i in range(workers // 2):
            p = base + lax.rem(me + i, workers // 2)
            copy = remote(src(p), dst.at[me], send, recv, {"ctx": first + p})

            @pl.when(p != slot)
            def _():
                copy.start()

            @pl.when(p == slot)
            def _():
                pltpu.make_async_copy(src(p), dst.at[me], recv).start()

    def send_group(base):
        to_workers(base, lambda p: tsend, taps_all, s_t, r_t)
        to_workers(base, lambda p: gsend.at[p], gpad, s_g, r_g)
        to_workers(base, lambda p: vsend.at[p], vpad, s_v, r_v)

    across = lax.broadcasted_iota(jnp.int32, (block, block), 0)
    along = lax.broadcasted_iota(jnp.int32, (block, block), 1)
    flip[...] = jnp.where(across + along == block - 1, 1.0, 0.0).astype(bf16)

    fetches[0].wait()
    own_taps = jnp.broadcast_to(taps_ref[...].astype(f32).reshape(1, block), (16, block)).astype(bf16)
    tsend[...] = jnp.dot(own_taps, flip[...], preferred_element_type=f32)[:1]
    fetches[1].wait()
    fetches[2].wait()
    grad_mid = (cot_ref[...].astype(f32) * gating_ref[...].astype(f32)).astype(bf16)
    gsend[...] = grad_mid.astype(f32).T.astype(bf16).reshape(workers, rows, block)
    fetches[3].wait()
    vsend[...] = (
        lax.dot_general(signal_ref[...], flip[...], TN, preferred_element_type=f32)
        .astype(bf16)
        .reshape(workers, rows, block)
    )

    def entered(core, group):
        @pl.when(ch == core)
        def _():
            pl.semaphore_wait(barrier, workers + 1 - group.astype(jnp.int32))
            pl.semaphore_signal(heard, inc=1, device_id={"ch": mate})

        @pl.when(ch != core)
        def _():
            pl.semaphore_wait(heard, 1)

    entered(0, near)
    send_group(0)
    entered(1, far)
    send_group(workers // 2)

    def at(k, size):
        return k * size if isinstance(k, int) else pl.multiple_of(k * size, half)

    def table(k):
        start = at(n - k, block)
        upper = toep[:, pl.ds(start, block)]
        lower = toep[:, pl.ds(start - half if isinstance(k, int) else pl.multiple_of(start - half, half), block)]
        return jnp.concatenate([upper, lower], axis=0)

    def over(low, high, step):
        if unrolled:
            for k in range(low, high):
                step(k)
        else:
            lax.fori_loop(low, high, lambda k, _: (step(k), 0)[1], 0)

    def backward_step(k):
        if unrolled:
            term = jnp.dot(
                gpad[k:n].reshape(total - k * rows, block), table(k), preferred_element_type=f32
            )
            if k == 0:
                acc[...] = term
            else:
                acc[: total - k * rows] += term
        else:
            acc[:total] += jnp.dot(
                gpad[pl.ds(k, n)].reshape(total, block), table(k), preferred_element_type=f32
            )

    def forward_step(k):
        if unrolled:
            term = jnp.dot(
                vpad[: n - k].reshape(total - k * rows, block), table(k), preferred_element_type=f32
            )
            if k == 0:
                acc[...] = term
            else:
                acc[k * rows :] += term
        else:
            start = pl.multiple_of(k * rows, 16)
            acc[pl.ds(start, total)] += jnp.dot(
                vpad[...].reshape(total, block), table(k), preferred_element_type=f32
            )

    def lag_step(k):
        if unrolled:
            left, right = vpad[: n - k].reshape(total - k * rows, block), gpad[k:n].reshape(total - k * rows, block)
        else:
            left, right = vpad[...].reshape(total, block), gpad[pl.ds(k, n)].reshape(total, block)
        mlag[:, pl.ds(at(k, block), block)] = lax.dot_general(left, right, TN, preferred_element_type=f32)

    def fold(k):
        span = block + half
        start = at(k, block)
        later = start + half if unrolled else pl.multiple_of(start + half, half)
        part = mlag[:half, pl.ds(later, span)] + mlag[half:, pl.ds(start, span)]
        turned = pltpu.roll(part, 1, 1, stride=1, stride_axis=0)[:, half:]
        lsend[pl.ds(k, 1)] = jnp.sum(turned, axis=0, keepdims=True)[None]

    def to_all(src, dst, send, recv, skip):
        def step(d, _):
            q = lax.rem(me + d, n)
            copy = remote(src.at[q], dst.at[slot], send, recv, {"ctx": q})
            if skip:
                pl.when(q >= skip)(copy.start)
            else:
                copy.start()
            return 0

        if unrolled:
            for d in range(1, n):
                step(d, 0)
        else:
            lax.fori_loop(1, n, step, 0)
        pltpu.make_async_copy(src.at[me], dst.at[slot], recv).start()

    @pl.when(is_worker)
    def _():
        if not unrolled:
            gpad[n:] = jnp.zeros((n, rows, block), bf16)
        hpad[...] = jnp.zeros(hpad.shape, f32)
        mlag[:, n * block :] = jnp.zeros((block, block), f32)
        drain(taps_all, r_t)
        for j in range(n):
            start = half + (n - 1 - j) * block
            hpad[:, start : start + block] = taps_all[j]
        for j in range(n + 1):
            window = jnp.broadcast_to(hpad[:, j * block : (j + 1) * block + half], (half, block + half))
            turned = pltpu.roll(window, 1, 1, stride=1, stride_axis=0)
            toep[:, j * block : (j + 1) * block] = turned[:, half:].astype(bf16)
        drain(gpad.at[:n], r_g)
        pl.semaphore_signal(mate_in, inc=1, device_id={"ch": mate})
        if not unrolled:
            acc[...] = jnp.zeros(acc.shape, f32)
        over(0, n, backward_step)
        bsend[...] = acc[:total].astype(bf16).reshape(n, rows, block)
        to_all(bsend, bret, s_b, r_b, 0)

        drain(vpad, r_v)
        lag_step(0)
        lag_step(1)
        fold(0)
        where = ch * workers + slot

        def send_lag(q, own, other):
            remote(lsend.at[q], lret.at[where], own, r_l, {"ctx": q}).start()
            remote(lsend.at[q], lret.at[where], other, r_l, {"ctx": q, "ch": mate}).start()

        pl.semaphore_wait(mate_in, 1)
        send_lag(0, s_l0, s_lo0)
        ysend[0] = jnp.dot(vpad[0], table(0), preferred_element_type=f32).astype(bf16)
        remote(ysend.at[0], yret.at[slot], s_y0, r_y, {"ctx": 0}).start()

        if not unrolled:
            acc[...] = jnp.zeros(acc.shape, f32)
        over(0, n, forward_step)
        ysend[1:] = acc[rows:total].astype(bf16).reshape(n - 1, rows, block)
        to_all(ysend, yret, s_y, r_y, 1)

        over(2, n, lag_step)
        over(1, n, fold)

        def send_lags(d, _):
            q = d + (d >= me).astype(jnp.int32)
            send_lag(q, s_l, s_lo)
            return 0

        if unrolled:
            for d in range(1, n - 1):
                send_lags(d, 0)
        else:
            lax.fori_loop(1, n - 1, send_lags, 0)
        pltpu.make_async_copy(lsend.at[me], lret.at[where], r_l).start()
        remote(lsend.at[me], lret.at[where], s_lo, r_l, {"ch": mate}).start()

    drain(bret, r_b)
    gs_ref[...] = bret[...].reshape(width, block).astype(f32).T.astype(bf16)
    drain(yret, r_y)
    recomputed = lax.dot_general(flip[...], yret[...].reshape(width, block), NT, preferred_element_type=f32)
    gg_ref[...] = (cot_ref[...].astype(f32) * recomputed).astype(bf16)
    drain(lret, r_l)
    gt_ref[...] = jnp.sum(lret[...], axis=0) * norm

    @pl.when(is_worker)
    def _():
        drain(taps_all.at[: workers - 1], s_t)
        drain(gsend.at[: workers - 1], s_g)
        drain(vsend.at[: workers - 1], s_v)
        drain(bsend.at[: n - 1], s_b)
        drain(lsend.at[0], s_l0)
        drain(lsend.at[0], s_lo0)
        drain(lsend.at[: n - 2], s_l)
        drain(lsend.at[: n - 1], s_lo)
        drain(ysend.at[0], s_y0)
        drain(ysend.at[: n - 2], s_y)

    @pl.when(jnp.logical_not(is_worker))
    def _():
        drain(taps_all.at[:workers], s_t)
        drain(gsend, s_g)
        drain(vsend, s_v)


def store(gs_in, gg_in, gt_in, gs_out, gg_out, gt_out, sems):
    copies = [
        pltpu.make_async_copy(src, dst, sems.at[i])
        for i, (src, dst) in enumerate(((gs_in, gs_out), (gg_in, gg_out), (gt_in, gt_out)))
    ]
    for copy in copies:
        copy.start()
    for copy in copies:
        copy.wait()


def body(signal, gating, filter_taps, cotangent):
    block, width = signal.shape
    n = lax.axis_size("ctx")
    pieces = lax.axis_size("ch")
    workers = WORKERS
    first = (n - workers) // 2
    rows = width // workers
    norm = 1.0 / math.sqrt(width * pieces * block * n)
    pad = 0 if n <= 16 else n
    hbm = pl.BlockSpec(memory_space=pltpu.HBM)
    vmem = pl.BlockSpec(memory_space=pltpu.VMEM)
    dma = pltpu.SemaphoreType.DMA
    results = (
        pltpu.VMEM((block, width), bf16),
        pltpu.VMEM((block, width), bf16),
        pltpu.VMEM((1, block), f32),
    )
    outputs = pl.pallas_call(
        functools.partial(kernel, n, workers, first, norm),
        out_shape=results,
        in_specs=[hbm] * 4,
        out_specs=(vmem,) * 3,
        scratch_shapes=[
            pltpu.VMEM((block, width), bf16),
            pltpu.VMEM((block, width), bf16),
            pltpu.VMEM((block,), bf16),
            pltpu.VMEM((block, width), bf16),
            pltpu.VMEM((block, block), bf16),
            pltpu.VMEM((1, block), f32),
            pltpu.VMEM((workers, rows, block), bf16),
            pltpu.VMEM((workers, rows, block), bf16),
            pltpu.VMEM((n, 1, block), f32),
            pltpu.VMEM((n + pad, rows, block), bf16),
            pltpu.VMEM((n, rows, block), bf16),
            pltpu.VMEM((n, rows, block), bf16),
            pltpu.VMEM((n, rows, block), bf16),
            pltpu.VMEM((n, 1, block), f32),
            pltpu.VMEM((workers, rows, block), bf16),
            pltpu.VMEM((workers, rows, block), bf16),
            pltpu.VMEM((pieces * workers, 1, block), f32),
            pltpu.VMEM((1, (n + 1) * block + block // 2), f32),
            pltpu.VMEM((block // 2, (n + 1) * block), bf16),
            pltpu.VMEM(((n + pad) * rows, block), f32),
            pltpu.VMEM((block, (n + 1) * block), f32),
        ]
        + [dma] * 16
        + [dma((4,)), pltpu.SemaphoreType.REGULAR, pltpu.SemaphoreType.REGULAR],
        compiler_params=pltpu.CompilerParams(
            collective_id=0, has_side_effects=True, vmem_limit_bytes=60 * 1024 * 1024
        ),
    )(signal, gating, filter_taps, cotangent)
    outputs = [pltpu.with_memory_space_constraint(o, pltpu.VMEM) for o in outputs]
    grad_signal, grad_gating, grad_taps = pl.pallas_call(
        store,
        out_shape=(
            jax.ShapeDtypeStruct((block, width), bf16),
            jax.ShapeDtypeStruct((block, width), bf16),
            jax.ShapeDtypeStruct((1, block), f32),
        ),
        in_specs=[vmem] * 3,
        out_specs=(hbm,) * 3,
        scratch_shapes=[dma((3,))],
    )(*outputs)
    return (grad_signal, grad_gating, grad_taps.reshape(block))


def solution(mesh):
    in_specs = (P("ctx", "ch"), P("ctx", "ch"), P("ctx"), P("ctx", "ch"))
    out_specs = (P("ctx", "ch"), P("ctx", "ch"), P("ctx"))
    return jax.shard_map(body, mesh=mesh, in_specs=in_specs, out_specs=out_specs, check_vma=False)
```

```python
import functools
import math

import jax
import jax.numpy as jnp
from jax import lax
from jax.experimental import pallas as pl
from jax.experimental.pallas import tpu as pltpu
from jax.sharding import PartitionSpec as P

WORKERS = 8
ORDER = (3, 1, 2, 0)
STEP = 5
f32 = jnp.float32
bf16 = jnp.bfloat16
NT = (((1,), (1,)), ((), ()))
TN = (((0,), (0,)), ((), ()))


def kernel(
    n, workers, first, norm,
    signal_hbm, gating_hbm, taps_hbm, cot_hbm,
    gs_ref, gg_ref, gt_ref,
    signal_ref, gating_ref, taps_ref, cot_ref, flip,
    tsend, gsend, vsend, taps_all, gpad, vpad,
    ysend, bsend, lsend, yret, bret, lret,
    hpad, toep, acc, mlag,
    s_t, s_g, s_v, s_y0, s_y, s_b, s_l0, s_lo0, s_l, s_lo,
    r_t, r_g, r_v, r_y, r_b, r_l, s_in, mate_in, heard,
):
    block, width = signal_ref.shape
    half = block // 2
    rows = width // workers
    total = n * rows
    unrolled = n <= 16
    me = lax.axis_index("ctx")
    ch = lax.axis_index("ch")
    mate = 1 - ch
    slot = me - first
    is_worker = jnp.logical_and(me >= first, me < first + workers)

    barrier = pltpu.get_barrier_semaphore()

    near = is_worker & (slot < workers // 2)
    far = is_worker & (slot >= workers // 2)

    def greet(core):
        for d in range(1, n):
            pl.semaphore_signal(barrier, inc=1, device_id={"ctx": lax.rem(me + d, n), "ch": core})
        pl.when(ch != core)(lambda: pl.semaphore_signal(barrier, inc=1, device_id={"ch": core}))

    pl.semaphore_signal(barrier, inc=1, device_id={"ch": mate})
    pl.when(near)(lambda: greet(0))
    pl.when(far)(lambda: greet(1))

    fetches = [
        pltpu.make_async_copy(src, dst, s_in.at[i])
        for i, (src, dst) in enumerate(
            ((taps_hbm, taps_ref), (cot_hbm, cot_ref), (gating_hbm, gating_ref), (signal_hbm, signal_ref))
        )
    ]
    for fetch in fetches:
        fetch.start()

    def remote(src, dst, send, recv, where):
        return pltpu.make_async_remote_copy(src_ref=src, dst_ref=dst, send_sem=send, recv_sem=recv, device_id=where)

    def drain(ref, sem):
        pltpu.make_async_copy(ref, ref, sem).wait()

    bits = [(1 - 2 * (me // 2**i % 2)) * 2**i for i in range((n - 1).bit_length())]

    def other(step):
        if n & (n - 1):
            return lax.rem(me + step, n)
        where = me
        for i, bit in enumerate(bits):
            where = where + (step // 2**i % 2) * bit
        return where

    def to_workers(base, src, dst, send, recv):
        for i in ORDER:
            p = base + lax.rem(other(i), workers // 2)
            copy = remote(src(p), dst.at[me], send, recv, {"ctx": first + p})

            @pl.when(p != slot)
            def _():
                copy.start()

            @pl.when(p == slot)
            def _():
                pltpu.make_async_copy(src(p), dst.at[me], recv).start()

    def send_group(base):
        to_workers(base, lambda p: tsend, taps_all, s_t, r_t)
        to_workers(base, lambda p: gsend.at[p], gpad, s_g, r_g)

    def send_late(base):
        to_workers(base, lambda p: vsend.at[p], vpad, s_v, r_v)

    across = lax.broadcasted_iota(jnp.int32, (block, block), 0)
    along = lax.broadcasted_iota(jnp.int32, (block, block), 1)
    flip[...] = jnp.where(across + along == block - 1, 1.0, 0.0).astype(bf16)

    fetches[0].wait()
    own_taps = jnp.broadcast_to(taps_ref[...].astype(f32).reshape(1, block), (16, block)).astype(bf16)
    tsend[...] = jnp.dot(own_taps, flip[...], preferred_element_type=f32)[:1]
    fetches[1].wait()
    fetches[2].wait()
    grad_mid = (cot_ref[...].astype(f32) * gating_ref[...].astype(f32)).astype(bf16)
    gsend[...] = grad_mid.astype(f32).T.astype(bf16).reshape(workers, rows, block)
    fetches[3].wait()
    vsend[...] = (
        lax.dot_general(signal_ref[...], flip[...], TN, preferred_element_type=f32)
        .astype(bf16)
        .reshape(workers, rows, block)
    )

    def entered(core, group):
        @pl.when(ch == core)
        def _():
            pl.semaphore_wait(barrier, workers + 1 - group.astype(jnp.int32))
            pl.semaphore_signal(heard, inc=1, device_id={"ch": mate})

        @pl.when(ch != core)
        def _():
            pl.semaphore_wait(heard, 1)

    entered(0, near)
    send_group(0)
    entered(1, far)
    send_group(workers // 2)
    send_late(0)
    send_late(workers // 2)

    def at(k, size):
        return k * size if isinstance(k, int) else pl.multiple_of(k * size, half)

    def table(k):
        start = at(n - k, block)
        upper = toep[:, pl.ds(start, block)]
        lower = toep[:, pl.ds(start - half if isinstance(k, int) else pl.multiple_of(start - half, half), block)]
        return jnp.concatenate([upper, lower], axis=0)

    def over(low, high, step):
        if unrolled:
            for k in range(low, high):
                step(k)
        else:
            lax.fori_loop(low, high, lambda k, _: (step(k), 0)[1], 0)

    def backward_step(k):
        if unrolled:
            term = jnp.dot(
                gpad[k:n].reshape(total - k * rows, block), table(k), preferred_element_type=f32
            )
            if k == 0:
                acc[...] = term
            else:
                acc[: total - k * rows] += term
        else:
            acc[:total] += jnp.dot(
                gpad[pl.ds(k, n)].reshape(total, block), table(k), preferred_element_type=f32
            )

    def forward_step(k):
        if unrolled:
            term = jnp.dot(
                vpad[: n - k].reshape(total - k * rows, block), table(k), preferred_element_type=f32
            )
            if k == 0:
                acc[...] = term
            else:
                acc[k * rows :] += term
        else:
            start = pl.multiple_of(k * rows, 16)
            acc[pl.ds(start, total)] += jnp.dot(
                vpad[...].reshape(total, block), table(k), preferred_element_type=f32
            )

    def lag_step(k):
        if unrolled:
            left, right = vpad[: n - k].reshape(total - k * rows, block), gpad[k:n].reshape(total - k * rows, block)
        else:
            left, right = vpad[...].reshape(total, block), gpad[pl.ds(k, n)].reshape(total, block)
        mlag[:, pl.ds(at(k, block), block)] = lax.dot_general(left, right, TN, preferred_element_type=f32)

    def fold(k):
        span = block + half
        start = at(k, block)
        later = start + half if unrolled else pl.multiple_of(start + half, half)
        part = mlag[:half, pl.ds(later, span)] + mlag[half:, pl.ds(start, span)]
        turned = pltpu.roll(part, 1, 1, stride=1, stride_axis=0)[:, half:]
        lsend[pl.ds(k, 1)] = jnp.sum(turned, axis=0, keepdims=True)[None]

    def to_all(src, dst, send, recv, skip):
        def step(d, _):
            q = other(STEP * d % n)
            copy = remote(src.at[q], dst.at[slot], send, recv, {"ctx": q})
            if skip:
                pl.when(q >= skip)(copy.start)
            else:
                copy.start()
            return 0

        if unrolled:
            for d in range(1, n):
                step(d, 0)
        else:
            lax.fori_loop(1, n, step, 0)
        pltpu.make_async_copy(src.at[me], dst.at[slot], recv).start()

    @pl.when(is_worker)
    def _():
        if not unrolled:
            gpad[n:] = jnp.zeros((n, rows, block), bf16)
        hpad[...] = jnp.zeros(hpad.shape, f32)
        mlag[:, n * block :] = jnp.zeros((block, block), f32)
        drain(taps_all, r_t)
        for j in range(n):
            start = half + (n - 1 - j) * block
            hpad[:, start : start + block] = taps_all[j]
        for j in range(n + 1):
            window = jnp.broadcast_to(hpad[:, j * block : (j + 1) * block + half], (half, block + half))
            turned = pltpu.roll(window, 1, 1, stride=1, stride_axis=0)
            toep[:, j * block : (j + 1) * block] = turned[:, half:].astype(bf16)
        drain(gpad.at[:n], r_g)
        pl.semaphore_signal(mate_in, inc=1, device_id={"ch": mate})
        if not unrolled:
            acc[...] = jnp.zeros(acc.shape, f32)
        @pl.when(me >= 0)
        def _():
            over(0, n, backward_step)
            bsend[...] = acc[:total].astype(bf16).reshape(n, rows, block)

        to_all(bsend, bret, s_b, r_b, 0)

        drain(vpad, r_v)
        lag_step(0)
        lag_step(1)
        fold(0)
        where = ch * workers + slot

        def send_lag(q, own, other):
            remote(lsend.at[q], lret.at[where], own, r_l, {"ctx": q}).start()
            remote(lsend.at[q], lret.at[where], other, r_l, {"ctx": q, "ch": mate}).start()

        pl.semaphore_wait(mate_in, 1)
        send_lag(0, s_l0, s_lo0)
        ysend[0] = jnp.dot(vpad[0], table(0), preferred_element_type=f32).astype(bf16)
        remote(ysend.at[0], yret.at[slot], s_y0, r_y, {"ctx": 0}).start()

        if not unrolled:
            acc[...] = jnp.zeros(acc.shape, f32)
        @pl.when(me >= 0)
        def _():
            over(0, n, forward_step)
            ysend[1:] = acc[rows:total].astype(bf16).reshape(n - 1, rows, block)

        to_all(ysend, yret, s_y, r_y, 1)

        over(2, n, lag_step)
        over(1, n, fold)

        def send_lags(d, _):
            q = d + (d >= me).astype(jnp.int32)
            send_lag(q, s_l, s_lo)
            return 0

        if unrolled:
            for d in range(1, n - 1):
                send_lags(d, 0)
        else:
            lax.fori_loop(1, n - 1, send_lags, 0)
        pltpu.make_async_copy(lsend.at[me], lret.at[where], r_l).start()
        remote(lsend.at[me], lret.at[where], s_lo, r_l, {"ch": mate}).start()

    drain(bret, r_b)
    gs_ref[...] = bret[...].reshape(width, block).astype(f32).T.astype(bf16)
    drain(yret, r_y)
    recomputed = lax.dot_general(flip[...], yret[...].reshape(width, block), NT, preferred_element_type=f32)
    gg_ref[...] = (cot_ref[...].astype(f32) * recomputed).astype(bf16)
    drain(lret, r_l)
    gt_ref[...] = jnp.sum(lret[...], axis=0) * norm

    @pl.when(is_worker)
    def _():
        drain(taps_all.at[: workers - 1], s_t)
        drain(gsend.at[: workers - 1], s_g)
        drain(vsend.at[: workers - 1], s_v)
        drain(bsend.at[: n - 1], s_b)
        drain(lsend.at[0], s_l0)
        drain(lsend.at[0], s_lo0)
        drain(lsend.at[: n - 2], s_l)
        drain(lsend.at[: n - 1], s_lo)
        drain(ysend.at[0], s_y0)
        drain(ysend.at[: n - 2], s_y)

    @pl.when(jnp.logical_not(is_worker))
    def _():
        drain(taps_all.at[:workers], s_t)
        drain(gsend, s_g)
        drain(vsend, s_v)


def store(gs_in, gg_in, gt_in, gs_out, gg_out, gt_out, sems):
    copies = [
        pltpu.make_async_copy(src, dst, sems.at[i])
        for i, (src, dst) in enumerate(((gs_in, gs_out), (gg_in, gg_out), (gt_in, gt_out)))
    ]
    for copy in copies:
        copy.start()
    for copy in copies:
        copy.wait()


def body(signal, gating, filter_taps, cotangent):
    block, width = signal.shape
    n = lax.axis_size("ctx")
    pieces = lax.axis_size("ch")
    workers = WORKERS
    first = (n - workers) // 2
    rows = width // workers
    norm = 1.0 / math.sqrt(width * pieces * block * n)
    pad = 0 if n <= 16 else n
    hbm = pl.BlockSpec(memory_space=pltpu.HBM)
    vmem = pl.BlockSpec(memory_space=pltpu.VMEM)
    dma = pltpu.SemaphoreType.DMA
    results = (
        pltpu.VMEM((block, width), bf16),
        pltpu.VMEM((block, width), bf16),
        pltpu.VMEM((1, block), f32),
    )
    outputs = pl.pallas_call(
        functools.partial(kernel, n, workers, first, norm),
        out_shape=results,
        in_specs=[hbm] * 4,
        out_specs=(vmem,) * 3,
        scratch_shapes=[
            pltpu.VMEM((block, width), bf16),
            pltpu.VMEM((block, width), bf16),
            pltpu.VMEM((block,), bf16),
            pltpu.VMEM((block, width), bf16),
            pltpu.VMEM((block, block), bf16),
            pltpu.VMEM((1, block), f32),
            pltpu.VMEM((workers, rows, block), bf16),
            pltpu.VMEM((workers, rows, block), bf16),
            pltpu.VMEM((n, 1, block), f32),
            pltpu.VMEM((n + pad, rows, block), bf16),
            pltpu.VMEM((n, rows, block), bf16),
            pltpu.VMEM((n, rows, block), bf16),
            pltpu.VMEM((n, rows, block), bf16),
            pltpu.VMEM((n, 1, block), f32),
            pltpu.VMEM((workers, rows, block), bf16),
            pltpu.VMEM((workers, rows, block), bf16),
            pltpu.VMEM((pieces * workers, 1, block), f32),
            pltpu.VMEM((1, (n + 1) * block + block // 2), f32),
            pltpu.VMEM((block // 2, (n + 1) * block), bf16),
            pltpu.VMEM(((n + pad) * rows, block), f32),
            pltpu.VMEM((block, (n + 1) * block), f32),
        ]
        + [dma] * 16
        + [dma((4,)), pltpu.SemaphoreType.REGULAR, pltpu.SemaphoreType.REGULAR],
        compiler_params=pltpu.CompilerParams(
            collective_id=0, has_side_effects=True, vmem_limit_bytes=60 * 1024 * 1024
        ),
    )(signal, gating, filter_taps, cotangent)
    outputs = [pltpu.with_memory_space_constraint(o, pltpu.VMEM) for o in outputs]
    grad_signal, grad_gating, grad_taps = pl.pallas_call(
        store,
        out_shape=(
            jax.ShapeDtypeStruct((block, width), bf16),
            jax.ShapeDtypeStruct((block, width), bf16),
            jax.ShapeDtypeStruct((1, block), f32),
        ),
        in_specs=[vmem] * 3,
        out_specs=(hbm,) * 3,
        scratch_shapes=[dma((3,))],
    )(*outputs)
    return (grad_signal, grad_gating, grad_taps.reshape(block))


def solution(mesh):
    in_specs = (P("ctx", "ch"), P("ctx", "ch"), P("ctx"), P("ctx", "ch"))
    out_specs = (P("ctx", "ch"), P("ctx", "ch"), P("ctx"))
    return jax.shard_map(body, mesh=mesh, in_specs=in_specs, out_specs=out_specs, check_vma=False)
```

```python
import functools
import math

import jax
import jax.numpy as jnp
from jax import lax
from jax.experimental import pallas as pl
from jax.experimental.pallas import tpu as pltpu
from jax.sharding import PartitionSpec as P

WORKERS = 8
ORDER = (3, 1, 2, 0)
OUT = (7, 11, 5, 9, 6, 10, 4, 8, 15, 3, 13, 1, 14, 2, 12)
f32 = jnp.float32
bf16 = jnp.bfloat16
NT = (((1,), (1,)), ((), ()))
TN = (((0,), (0,)), ((), ()))


def kernel(
    n, workers, first, edge, norm,
    signal_hbm, gating_hbm, taps_hbm, cot_hbm,
    gs_ref, gg_ref, gt_ref,
    signal_ref, gating_ref, taps_ref, cot_ref, flip,
    tsend, gsend, vsend, taps_all, gpad, vpad,
    ysend, bsend, lsend, yret, bret, lret,
    hpad, toep, acc, mlag,
    taps_few, nv, nd, nysend, nbsend, nyret, nbret, nlret,
    s_t, s_g, s_v, s_y, s_b, s_l0, s_lo0, s_l, s_lo, s_nt, s_nv, s_nd,
    r_t, r_g, r_v, r_y, r_b, r_l, r_nt, r_nv, r_nd, r_ny, r_nb, r_nl,
    s_in, mate_in, heard,
):
    block, width = signal_ref.shape
    half = block // 2
    rows = width // workers
    total = n * rows
    unrolled = n <= 16
    me = lax.axis_index("ctx")
    ch = lax.axis_index("ch")
    mate = 1 - ch
    slot = me - first
    is_worker = jnp.logical_and(me >= first, me < first + workers)
    is_edge = jnp.logical_not(is_worker)
    low = me < edge
    high = me >= n - edge
    lead = max(edge, 1)

    barrier = pltpu.get_barrier_semaphore()

    near = is_worker & (slot < workers // 2)
    far = is_worker & (slot >= workers // 2)

    def greet(core):
        for d in range(1, n):
            pl.semaphore_signal(barrier, inc=1, device_id={"ctx": lax.rem(me + d, n), "ch": core})
        pl.when(ch != core)(lambda: pl.semaphore_signal(barrier, inc=1, device_id={"ch": core}))

    bits = [(1 - 2 * (me // 2**i % 2)) * 2**i for i in range((n - 1).bit_length())]

    def other(step):
        if n & (n - 1):
            return lax.rem(me + step, n)
        where = me
        for i, bit in enumerate(bits):
            where = where + (step // 2**i % 2) * bit
        return where

    pl.semaphore_signal(barrier, inc=1, device_id={"ch": mate})
    if edge:
        @pl.when(is_edge)
        def _():
            for i in range(1, edge):
                pl.semaphore_signal(barrier, inc=1, device_id={"ctx": other(i)})

    pl.when(near)(lambda: greet(0))
    pl.when(far)(lambda: greet(1))

    fetches = [
        pltpu.make_async_copy(src, dst, s_in.at[i])
        for i, (src, dst) in enumerate(
            ((taps_hbm, taps_ref), (cot_hbm, cot_ref), (gating_hbm, gating_ref), (signal_hbm, signal_ref))
        )
    ]
    for fetch in fetches:
        fetch.start()

    def remote(src, dst, send, recv, where):
        return pltpu.make_async_remote_copy(src_ref=src, dst_ref=dst, send_sem=send, recv_sem=recv, device_id=where)

    def drain(ref, sem):
        pltpu.make_async_copy(ref, ref, sem).wait()

    def to_workers(base, src, dst, send, recv):
        for i in ORDER:
            p = base + lax.rem(other(i), workers // 2)
            copy = remote(src(p), dst.at[me], send, recv, {"ctx": first + p})

            @pl.when(p != slot)
            def _():
                copy.start()

            @pl.when(p == slot)
            def _():
                pltpu.make_async_copy(src(p), dst.at[me], recv).start()

    def send_group(base):
        to_workers(base, lambda p: tsend, taps_all, s_t, r_t)

        @pl.when(me >= edge)
        def _():
            to_workers(base, lambda p: gsend.at[p], gpad, s_g, r_g)

        if edge:
            @pl.when(low)
            def _():
                to_workers(base, lambda p: vsend.at[p], vpad, s_v, r_v)

    def send_late(base):
        to_workers(base, lambda p: vsend.at[p], vpad, s_v, r_v)

    across = lax.broadcasted_iota(jnp.int32, (block, block), 0)
    along = lax.broadcasted_iota(jnp.int32, (block, block), 1)
    flip[...] = jnp.where(across + along == block - 1, 1.0, 0.0).astype(bf16)

    fetches[0].wait()
    own_taps = jnp.broadcast_to(taps_ref[...].astype(f32).reshape(1, block), (16, block)).astype(bf16)
    tsend[...] = jnp.dot(own_taps, flip[...], preferred_element_type=f32)[:1]
    fetches[1].wait()
    fetches[2].wait()
    grad_mid = (cot_ref[...].astype(f32) * gating_ref[...].astype(f32)).astype(bf16)
    gsend[...] = grad_mid.astype(f32).T.astype(bf16).reshape(workers, rows, block)
    fetches[3].wait()
    vsend[...] = (
        lax.dot_general(signal_ref[...], flip[...], TN, preferred_element_type=f32)
        .astype(bf16)
        .reshape(workers, rows, block)
    )

    def entered(core, group):
        @pl.when(ch == core)
        def _():
            extra = is_edge.astype(jnp.int32) * (edge - 1) if edge else 0
            pl.semaphore_wait(barrier, workers + 1 - group.astype(jnp.int32) + extra)
            pl.semaphore_signal(heard, inc=1, device_id={"ch": mate})

        @pl.when(ch != core)
        def _():
            pl.semaphore_wait(heard, 1)

    entered(0, near)
    send_group(0)
    entered(1, far)
    send_group(workers // 2)

    @pl.when(jnp.logical_and(me >= edge, me < n - edge))
    def _():
        send_late(0)
        send_late(workers // 2)

    if edge:
        per = workers // edge
        base = me - me % edge
        place = me % edge

        def among(src, dst, send, recv):
            for i in range(1, edge):
                q = other(i)
                remote(src(q - base), dst.at[place], send, recv, {"ctx": q}).start()
            pltpu.make_async_copy(src(place), dst.at[place], recv).start()

        @pl.when(is_edge)
        def _():
            among(lambda p: vsend.at[pl.ds(p * per, per)], nv, s_nv, r_nv)
            among(lambda p: gsend.at[pl.ds(p * per, per)], nd, s_nd, r_nd)

    def at(k, size):
        return k * size if isinstance(k, int) else pl.multiple_of(k * size, half)

    def build(taps, m):
        for j in range(m):
            start = half + (m - 1 - j) * block
            hpad[:, start : start + block] = taps[j]
        for j in range(m + 1):
            window = jnp.broadcast_to(hpad[:, j * block : (j + 1) * block + half], (half, block + half))
            turned = pltpu.roll(window, 1, 1, stride=1, stride_axis=0)
            toep[:, j * block : (j + 1) * block] = turned[:, half:].astype(bf16)

    def table(k, m=n):
        start = at(m - k, block)
        upper = toep[:, pl.ds(start, block)]
        lower = toep[:, pl.ds(start - half if isinstance(k, int) else pl.multiple_of(start - half, half), block)]
        return jnp.concatenate([upper, lower], axis=0)

    def over(low_k, high_k, step):
        if unrolled:
            for k in range(low_k, high_k):
                step(k)
        else:
            lax.fori_loop(low_k, high_k, lambda k, _: (step(k), 0)[1], 0)

    def span_of(k):
        return max(0, edge - k), min(n - edge, n - k)

    def flat(ref, start, stop):
        part = ref[start:stop]
        return part.reshape(-1, block)

    def products(src, shift_in, shift_out):
        for k in [edge] + [k for k in range(n) if k != edge]:
            start, stop = span_of(k)
            term = jnp.dot(
                flat(src, start + k * shift_in, stop + k * shift_in), table(k), preferred_element_type=f32
            )
            where = pl.ds((start + k * shift_out) * rows, (stop - start) * rows)
            if k == edge:
                acc[where] = term
            else:
                acc[where] += term

    def backward_step(k):
        acc[:total] += jnp.dot(
            gpad[pl.ds(k, n)].reshape(total, block), table(k), preferred_element_type=f32
        )

    def forward_step(k):
        start = pl.multiple_of(k * rows, 16)
        acc[pl.ds(start, total)] += jnp.dot(
            vpad[...].reshape(total, block), table(k), preferred_element_type=f32
        )

    def lag_step(k):
        if unrolled:
            start, stop = span_of(k)
            left, right = flat(vpad, start, stop), flat(gpad, start + k, stop + k)
        else:
            left, right = vpad[...].reshape(total, block), gpad[pl.ds(k, n)].reshape(total, block)
        mlag[:, pl.ds(at(k, block), block)] = lax.dot_general(left, right, TN, preferred_element_type=f32)

    def fold(k):
        span = block + half
        start = at(k, block)
        later = start + half if unrolled else pl.multiple_of(start + half, half)
        part = mlag[:half, pl.ds(later, span)] + mlag[half:, pl.ds(start, span)]
        turned = pltpu.roll(part, 1, 1, stride=1, stride_axis=0)[:, half:]
        lsend[pl.ds(k, 1)] = jnp.sum(turned, axis=0, keepdims=True)[None]

    def to_all(src, dst, send, recv, start, stop):
        def step(d, _):
            q = other(d)
            copy = remote(src.at[q], dst.at[slot], send, recv, {"ctx": q})
            if start == 0 and stop == n:
                copy.start()
            else:
                pl.when(jnp.logical_and(q >= start, q < stop))(copy.start)
            return 0

        if n == 16:
            for d in OUT:
                step(d, 0)
        else:
            lax.fori_loop(1, n, step, 0)
        pltpu.make_async_copy(src.at[me], dst.at[slot], recv).start()

    apart = pl.when(me >= 0)

    @pl.when(is_worker)
    def _():
        if not unrolled:
            gpad[n:] = jnp.zeros((n, rows, block), bf16)
        hpad[...] = jnp.zeros(hpad.shape, f32)
        mlag[:, n * block :] = jnp.zeros((block, block), f32)
        drain(taps_all, r_t)
        if edge:
            target = slot + (slot // edge) * (n - workers)
            remote(taps_all.at[:edge], taps_few, s_nt, r_nt, {"ctx": target}).start()
        build(taps_all, n)
        drain(gpad.at[edge:n], r_g)
        pl.semaphore_signal(mate_in, inc=1, device_id={"ch": mate})

        @apart
        def _():
            if unrolled:
                products(gpad, 1, 0)
            else:
                acc[...] = jnp.zeros(acc.shape, f32)
                over(0, n, backward_step)
            bsend[: n - edge] = acc[: (n - edge) * rows].astype(bf16).reshape(n - edge, rows, block)

        to_all(bsend, bret, s_b, r_b, 0, n - edge)

        drain(vpad.at[: n - edge], r_v)

        @apart
        def _():
            over(0, lead + 1, lag_step)
            over(0, lead, fold)

        where = ch * workers + slot

        def send_lag(q, own, across):
            remote(lsend.at[q], lret.at[where], own, r_l, {"ctx": q}).start()
            remote(lsend.at[q], lret.at[where], across, r_l, {"ctx": q, "ch": mate}).start()

        pl.semaphore_wait(mate_in, 1)
        for q in range(lead):
            send_lag(q, s_l0, s_lo0)

        @apart
        def _():
            if unrolled:
                products(vpad, 0, 1)
            else:
                acc[...] = jnp.zeros(acc.shape, f32)
                over(0, n, forward_step)
            ysend[edge:] = acc[edge * rows : total].astype(bf16).reshape(n - edge, rows, block)

        to_all(ysend, yret, s_y, r_y, edge, n)

        @apart
        def _():
            over(lead + 1, n, lag_step)
            over(lead, n, fold)

        def send_lags(d, _):
            q = d + (d >= me).astype(jnp.int32)
            send_lag(q, s_l, s_lo)
            return 0

        if unrolled:
            for d in range(lead, n - 1):
                send_lags(d, 0)
        else:
            lax.fori_loop(lead, n - 1, send_lags, 0)
        pltpu.make_async_copy(lsend.at[me], lret.at[where], r_l).start()
        remote(lsend.at[me], lret.at[where], s_lo, r_l, {"ch": mate}).start()

    if edge:
        @pl.when(is_edge)
        def _():
            size = per * rows
            hpad[...] = jnp.zeros(hpad.shape, f32)
            mlag[:, edge * block : (edge + 1) * block] = jnp.zeros((block, block), f32)
            drain(taps_few, r_nt)
            pl.semaphore_signal(mate_in, inc=1, device_id={"ch": mate})
            build(taps_few, edge)
            drain(nv, r_nv)

            def near_products(src, shift_in, shift_out):
                for k in range(edge):
                    term = jnp.dot(
                        flat(src, k * shift_in, edge - k + k * shift_in), table(k, edge), preferred_element_type=f32
                    )
                    where = pl.ds(k * shift_out * size, (edge - k) * size)
                    if k == 0:
                        acc[where] = term
                    else:
                        acc[where] += term

            @apart
            def _():
                near_products(nv, 0, 1)
                nysend[...] = acc[: edge * size].astype(bf16).reshape(nysend.shape)

            among(lambda p: nysend.at[p], nyret, s_y, r_ny)
            drain(nd, r_nd)

            @apart
            def _():
                near_products(nd, 1, 0)
                nbsend[...] = acc[: edge * size].astype(bf16).reshape(nbsend.shape)

            among(lambda p: nbsend.at[p], nbret, s_b, r_nb)

            @apart
            def _():
                for k in range(edge):
                    mlag[:, k * block : (k + 1) * block] = lax.dot_general(
                        flat(nv, 0, edge - k), flat(nd, k, edge), TN, preferred_element_type=f32
                    )
                over(0, edge, fold)

            pl.semaphore_wait(mate_in, 1)
            where = (ch * 2 + high.astype(jnp.int32)) * edge + place
            for q in range(edge):
                copy = remote(lsend.at[q], nlret.at[where], s_l, r_nl, {"ctx": q})
                pl.when(me != q)(copy.start)
                remote(lsend.at[q], nlret.at[where], s_lo, r_nl, {"ctx": q, "ch": mate}).start()

            @pl.when(low)
            def _():
                pltpu.make_async_copy(lsend.at[me], nlret.at[where], r_nl).start()

    def put_signal(*parts):
        joined = sum(part[...].reshape(width, block).astype(f32) for part in parts)
        gs_ref[...] = joined.T.astype(bf16)

    def put_gating(*parts):
        recomputed = sum(
            lax.dot_general(flip[...], part[...].reshape(width, block), NT, preferred_element_type=f32)
            for part in parts
        )
        gg_ref[...] = (cot_ref[...].astype(f32) * recomputed).astype(bf16)

    def put_taps(*parts):
        gt_ref[...] = sum(jnp.sum(part[...], axis=0) for part in parts) * norm

    @pl.when(jnp.logical_and(me >= edge, me < n - edge))
    def _():
        drain(bret, r_b)
        put_signal(bret)
        drain(yret, r_y)
        put_gating(yret)
        drain(lret, r_l)
        put_taps(lret)

    if edge:
        @pl.when(low)
        def _():
            drain(nyret, r_ny)
            put_gating(nyret)
            drain(nbret, r_nb)
            drain(bret, r_b)
            put_signal(nbret, bret)
            drain(nlret, r_nl)
            drain(lret, r_l)
            put_taps(nlret, lret)

        @pl.when(high)
        def _():
            drain(nbret, r_nb)
            put_signal(nbret)
            drain(nyret, r_ny)
            drain(yret, r_y)
            put_gating(nyret, yret)
            drain(lret, r_l)
            put_taps(lret)

    @pl.when(is_worker)
    def _():
        drain(taps_all.at[: workers - 1], s_t)
        drain(gsend.at[: workers - 1], s_g)
        drain(vsend.at[: workers - 1], s_v)
        if edge:
            drain(taps_all.at[:edge], s_nt)
        drain(bsend.at[: n - edge - 1], s_b)
        drain(lsend.at[:lead], s_l0)
        drain(lsend.at[:lead], s_lo0)
        drain(lsend.at[: n - lead - 1], s_l)
        drain(lsend.at[: n - lead], s_lo)
        drain(ysend.at[: n - edge - 1], s_y)

    @pl.when(is_edge)
    def _():
        drain(taps_all.at[:workers], s_t)
        if edge:
            pl.when(high)(lambda: drain(gsend, s_g))
            pl.when(low)(lambda: drain(vsend, s_v))
            drain(nv.at[: edge - 1], s_nv)
            drain(nd.at[: edge - 1], s_nd)
            drain(nysend.at[: edge - 1], s_y)
            drain(nbsend.at[: edge - 1], s_b)
            pl.when(low)(lambda: drain(lsend.at[: edge - 1], s_l))
            pl.when(high)(lambda: drain(lsend.at[:edge], s_l))
            drain(lsend.at[:edge], s_lo)
        else:
            drain(gsend, s_g)
            drain(vsend, s_v)


def store(gs_in, gg_in, gt_in, gs_out, gg_out, gt_out, sems):
    copies = [
        pltpu.make_async_copy(src, dst, sems.at[i])
        for i, (src, dst) in enumerate(((gs_in, gs_out), (gg_in, gg_out), (gt_in, gt_out)))
    ]
    for copy in copies:
        copy.start()
    for copy in copies:
        copy.wait()


def body(signal, gating, filter_taps, cotangent):
    block, width = signal.shape
    n = lax.axis_size("ctx")
    pieces = lax.axis_size("ch")
    workers = WORKERS
    first = (n - workers) // 2
    rows = width // workers
    whole = n & (n - 1) == 0 and workers % 2 == 0 and first == workers // 2
    edge = first if whole else 0
    few = max(edge, 1)
    per = workers // few
    norm = 1.0 / math.sqrt(width * pieces * block * n)
    pad = 0 if n <= 16 else n
    hbm = pl.BlockSpec(memory_space=pltpu.HBM)
    vmem = pl.BlockSpec(memory_space=pltpu.VMEM)
    dma = pltpu.SemaphoreType.DMA
    results = (
        pltpu.VMEM((block, width), bf16),
        pltpu.VMEM((block, width), bf16),
        pltpu.VMEM((1, block), f32),
    )
    outputs = pl.pallas_call(
        functools.partial(kernel, n, workers, first, edge, norm),
        out_shape=results,
        in_specs=[hbm] * 4,
        out_specs=(vmem,) * 3,
        scratch_shapes=[
            pltpu.VMEM((block, width), bf16),
            pltpu.VMEM((block, width), bf16),
            pltpu.VMEM((block,), bf16),
            pltpu.VMEM((block, width), bf16),
            pltpu.VMEM((block, block), bf16),
            pltpu.VMEM((1, block), f32),
            pltpu.VMEM((workers, rows, block), bf16),
            pltpu.VMEM((workers, rows, block), bf16),
            pltpu.VMEM((n, 1, block), f32),
            pltpu.VMEM((n + pad, rows, block), bf16),
            pltpu.VMEM((n, rows, block), bf16),
            pltpu.VMEM((n, rows, block), bf16),
            pltpu.VMEM((n, rows, block), bf16),
            pltpu.VMEM((n, 1, block), f32),
            pltpu.VMEM((workers, rows, block), bf16),
            pltpu.VMEM((workers, rows, block), bf16),
            pltpu.VMEM((pieces * workers, 1, block), f32),
            pltpu.VMEM((1, (n + 1) * block + block // 2), f32),
            pltpu.VMEM((block // 2, (n + 1) * block), bf16),
            pltpu.VMEM(((n + pad) * rows, block), f32),
            pltpu.VMEM((block, (n + 1) * block), f32),
            pltpu.VMEM((few, 1, block), f32),
        ]
        + [pltpu.VMEM((few, per, rows, block), bf16)] * 6
        + [pltpu.VMEM((2 * pieces * few, 1, block), f32)]
        + [dma] * 24
        + [dma((4,)), pltpu.SemaphoreType.REGULAR, pltpu.SemaphoreType.REGULAR],
        compiler_params=pltpu.CompilerParams(
            collective_id=0, has_side_effects=True, vmem_limit_bytes=60 * 1024 * 1024
        ),
    )(signal, gating, filter_taps, cotangent)
    outputs = [pltpu.with_memory_space_constraint(o, pltpu.VMEM) for o in outputs]
    grad_signal, grad_gating, grad_taps = pl.pallas_call(
        store,
        out_shape=(
            jax.ShapeDtypeStruct((block, width), bf16),
            jax.ShapeDtypeStruct((block, width), bf16),
            jax.ShapeDtypeStruct((1, block), f32),
        ),
        in_specs=[vmem] * 3,
        out_specs=(hbm,) * 3,
        scratch_shapes=[dma((3,))],
    )(*outputs)
    return (grad_signal, grad_gating, grad_taps.reshape(block))


def solution(mesh):
    in_specs = (P("ctx", "ch"), P("ctx", "ch"), P("ctx"), P("ctx", "ch"))
    out_specs = (P("ctx", "ch"), P("ctx", "ch"), P("ctx"))
    return jax.shard_map(body, mesh=mesh, in_specs=in_specs, out_specs=out_specs, check_vma=False)
```

```python
import functools
import math

import jax
import jax.numpy as jnp
from jax import lax
from jax.experimental import pallas as pl
from jax.experimental.pallas import tpu as pltpu
from jax.sharding import PartitionSpec as P

WORKERS = 8
ORDER = (3, 1, 2, 0)
OUT = (7, 11, 5, 9, 6, 10, 4, 8, 15, 3, 13, 1, 14, 2, 12)
f32 = jnp.float32
bf16 = jnp.bfloat16
NT = (((1,), (1,)), ((), ()))
TN = (((0,), (0,)), ((), ()))


def kernel(
    n, workers, first, edge, norm,
    signal_hbm, gating_hbm, taps_hbm, cot_hbm,
    gs_ref, gg_ref, gt_ref,
    signal_ref, gating_ref, taps_ref, cot_ref, flip,
    tsend, gsend, vsend, taps_all, gpad, vpad,
    ysend, bsend, lsend, yret, bret, lret,
    hpad, toep, acc, mlag,
    taps_few, nv, nd, nysend, nbsend, nyret, nbret, few_lags,
    s_t, s_g, s_v, s_y, s_b, s_l0, s_lo0, s_l, s_lo, s_nt, s_nv, s_nd, s_nl,
    r_t, r_g, r_v, r_y, r_b, r_l, r_nt, r_nv, r_nd, r_ny, r_nb, r_nl,
    s_in, mate_in, heard,
):
    block, width = signal_ref.shape
    half = block // 2
    rows = width // workers
    total = n * rows
    unrolled = n <= 16
    me = lax.axis_index("ctx")
    ch = lax.axis_index("ch")
    mate = 1 - ch
    slot = me - first
    is_worker = jnp.logical_and(me >= first, me < first + workers)
    is_edge = jnp.logical_not(is_worker)
    low = me < edge
    high = me >= n - edge
    lead = max(edge, 1)

    barrier = pltpu.get_barrier_semaphore()

    near = is_worker & (slot < workers // 2)
    far = is_worker & (slot >= workers // 2)

    def greet(core):
        for d in range(1, n):
            pl.semaphore_signal(barrier, inc=1, device_id={"ctx": lax.rem(me + d, n), "ch": core})
        pl.when(ch != core)(lambda: pl.semaphore_signal(barrier, inc=1, device_id={"ch": core}))

    bits = [(1 - 2 * (me // 2**i % 2)) * 2**i for i in range((n - 1).bit_length())]

    def other(step):
        if n & (n - 1):
            return lax.rem(me + step, n)
        where = me
        for i, bit in enumerate(bits):
            where = where + (step // 2**i % 2) * bit
        return where

    pl.semaphore_signal(barrier, inc=1, device_id={"ch": mate})
    if edge:
        @pl.when(is_edge)
        def _():
            for i in range(1, edge):
                pl.semaphore_signal(barrier, inc=1, device_id={"ctx": other(i)})

    pl.when(near)(lambda: greet(0))
    pl.when(far)(lambda: greet(1))

    fetches = [
        pltpu.make_async_copy(src, dst, s_in.at[i])
        for i, (src, dst) in enumerate(
            ((taps_hbm, taps_ref), (cot_hbm, cot_ref), (gating_hbm, gating_ref), (signal_hbm, signal_ref))
        )
    ]
    for fetch in fetches:
        fetch.start()

    def remote(src, dst, send, recv, where):
        return pltpu.make_async_remote_copy(src_ref=src, dst_ref=dst, send_sem=send, recv_sem=recv, device_id=where)

    def drain(ref, sem):
        pltpu.make_async_copy(ref, ref, sem).wait()

    def to_workers(base, src, dst, send, recv):
        for i in ORDER:
            p = base + lax.rem(other(i), workers // 2)
            copy = remote(src(p), dst.at[me], send, recv, {"ctx": first + p})

            @pl.when(p != slot)
            def _():
                copy.start()

            @pl.when(p == slot)
            def _():
                pltpu.make_async_copy(src(p), dst.at[me], recv).start()

    def send_group(base):
        to_workers(base, lambda p: tsend, taps_all, s_t, r_t)

        @pl.when(me >= edge)
        def _():
            to_workers(base, lambda p: gsend.at[p], gpad, s_g, r_g)

        if edge:
            @pl.when(low)
            def _():
                to_workers(base, lambda p: vsend.at[p], vpad, s_v, r_v)

    def send_late(base):
        to_workers(base, lambda p: vsend.at[p], vpad, s_v, r_v)

    across = lax.broadcasted_iota(jnp.int32, (block, block), 0)
    along = lax.broadcasted_iota(jnp.int32, (block, block), 1)
    flip[...] = jnp.where(across + along == block - 1, 1.0, 0.0).astype(bf16)

    fetches[0].wait()
    own_taps = jnp.broadcast_to(taps_ref[...].astype(f32).reshape(1, block), (16, block)).astype(bf16)
    tsend[...] = jnp.dot(own_taps, flip[...], preferred_element_type=f32)[:1]
    fetches[1].wait()
    fetches[2].wait()
    grad_mid = (cot_ref[...].astype(f32) * gating_ref[...].astype(f32)).astype(bf16)
    gsend[...] = grad_mid.astype(f32).T.astype(bf16).reshape(workers, rows, block)
    fetches[3].wait()
    vsend[...] = (
        lax.dot_general(signal_ref[...], flip[...], TN, preferred_element_type=f32)
        .astype(bf16)
        .reshape(workers, rows, block)
    )

    def entered(core, group):
        @pl.when(ch == core)
        def _():
            extra = is_edge.astype(jnp.int32) * (edge - 1) if edge else 0
            pl.semaphore_wait(barrier, workers + 1 - group.astype(jnp.int32) + extra)
            pl.semaphore_signal(heard, inc=1, device_id={"ch": mate})

        @pl.when(ch != core)
        def _():
            pl.semaphore_wait(heard, 1)

    entered(0, near)
    send_group(0)
    entered(1, far)
    send_group(workers // 2)

    @pl.when(jnp.logical_and(me >= edge, me < n - edge))
    def _():
        send_late(0)
        send_late(workers // 2)

    if edge:
        per = workers // edge
        base = me - me % edge
        place = me % edge

        def among(src, dst, send, recv):
            for i in range(1, edge):
                q = other(i)
                remote(src(q - base), dst.at[place], send, recv, {"ctx": q}).start()
            pltpu.make_async_copy(src(place), dst.at[place], recv).start()

        @pl.when(is_edge)
        def _():
            pl.when(low)(lambda: among(lambda p: tsend, taps_few, s_nt, r_nt))
            among(lambda p: vsend.at[pl.ds(p * per, per)], nv, s_nv, r_nv)
            among(lambda p: gsend.at[pl.ds(p * per, per)], nd, s_nd, r_nd)

    def at(k, size):
        return k * size if isinstance(k, int) else pl.multiple_of(k * size, half)

    def build(taps, m):
        for j in range(m):
            start = half + (m - 1 - j) * block
            hpad[:, start : start + block] = taps[j]
        for j in range(m + 1):
            window = jnp.broadcast_to(hpad[:, j * block : (j + 1) * block + half], (half, block + half))
            turned = pltpu.roll(window, 1, 1, stride=1, stride_axis=0)
            toep[:, j * block : (j + 1) * block] = turned[:, half:].astype(bf16)

    def table(k, m=n):
        start = at(m - k, block)
        upper = toep[:, pl.ds(start, block)]
        lower = toep[:, pl.ds(start - half if isinstance(k, int) else pl.multiple_of(start - half, half), block)]
        return jnp.concatenate([upper, lower], axis=0)

    def over(low_k, high_k, step):
        if unrolled:
            for k in range(low_k, high_k):
                step(k)
        else:
            lax.fori_loop(low_k, high_k, lambda k, _: (step(k), 0)[1], 0)

    def span_of(k):
        return max(0, edge - k), min(n - edge, n - k)

    def flat(ref, start, stop):
        part = ref[start:stop]
        return part.reshape(-1, block)

    def products(src, shift_in, shift_out):
        for k in [edge] + [k for k in range(n) if k != edge]:
            start, stop = span_of(k)
            term = jnp.dot(
                flat(src, start + k * shift_in, stop + k * shift_in), table(k), preferred_element_type=f32
            )
            where = pl.ds((start + k * shift_out) * rows, (stop - start) * rows)
            if k == edge:
                acc[where] = term
            else:
                acc[where] += term

    def backward_step(k):
        acc[:total] += jnp.dot(
            gpad[pl.ds(k, n)].reshape(total, block), table(k), preferred_element_type=f32
        )

    def forward_step(k):
        start = pl.multiple_of(k * rows, 16)
        acc[pl.ds(start, total)] += jnp.dot(
            vpad[...].reshape(total, block), table(k), preferred_element_type=f32
        )

    def lag_step(k):
        if unrolled:
            start, stop = span_of(k)
            left, right = flat(vpad, start, stop), flat(gpad, start + k, stop + k)
        else:
            left, right = vpad[...].reshape(total, block), gpad[pl.ds(k, n)].reshape(total, block)
        mlag[:, pl.ds(at(k, block), block)] = lax.dot_general(left, right, TN, preferred_element_type=f32)

    def fold(k):
        span = block + half
        start = at(k, block)
        later = start + half if unrolled else pl.multiple_of(start + half, half)
        part = mlag[:half, pl.ds(later, span)] + mlag[half:, pl.ds(start, span)]
        turned = pltpu.roll(part, 1, 1, stride=1, stride_axis=0)[:, half:]
        lsend[pl.ds(k, 1)] = jnp.sum(turned, axis=0, keepdims=True)[None]

    def to_all(src, dst, send, recv, start, stop):
        def step(d, _):
            q = other(d)
            copy = remote(src.at[q], dst.at[slot], send, recv, {"ctx": q})
            if start == 0 and stop == n:
                copy.start()
            else:
                pl.when(jnp.logical_and(q >= start, q < stop))(copy.start)
            return 0

        if n == 16:
            for d in OUT:
                step(d, 0)
        else:
            lax.fori_loop(1, n, step, 0)
        pltpu.make_async_copy(src.at[me], dst.at[slot], recv).start()

    apart = pl.when(me >= 0)

    @pl.when(is_worker)
    def _():
        if not unrolled:
            gpad[n:] = jnp.zeros((n, rows, block), bf16)
        hpad[...] = jnp.zeros(hpad.shape, f32)
        mlag[:, n * block :] = jnp.zeros((block, block), f32)
        drain(taps_all, r_t)
        if edge:
            onward = remote(taps_all.at[:edge], taps_few, s_nt, r_nt, {"ctx": slot + n - workers})
            pl.when(far)(onward.start)
        build(taps_all, n)
        drain(gpad.at[edge:n], r_g)
        pl.semaphore_signal(mate_in, inc=1, device_id={"ch": mate})

        @apart
        def _():
            if unrolled:
                products(gpad, 1, 0)
            else:
                acc[...] = jnp.zeros(acc.shape, f32)
                over(0, n, backward_step)
            bsend[: n - edge] = acc[: (n - edge) * rows].astype(bf16).reshape(n - edge, rows, block)

        to_all(bsend, bret, s_b, r_b, 0, n - edge)

        drain(vpad.at[: n - edge], r_v)

        @apart
        def _():
            over(0, lead + 1, lag_step)
            over(0, lead, fold)

        if edge:
            drain(few_lags, r_nl)
            lsend[:edge] += few_lags[...]
        where = ch * workers + slot

        def send_lag(q, own, across):
            remote(lsend.at[q], lret.at[where], own, r_l, {"ctx": q}).start()
            remote(lsend.at[q], lret.at[where], across, r_l, {"ctx": q, "ch": mate}).start()

        pl.semaphore_wait(mate_in, 1)
        for q in range(lead):
            send_lag(q, s_l0, s_lo0)

        @apart
        def _():
            if unrolled:
                products(vpad, 0, 1)
            else:
                acc[...] = jnp.zeros(acc.shape, f32)
                over(0, n, forward_step)
            ysend[edge:] = acc[edge * rows : total].astype(bf16).reshape(n - edge, rows, block)

        to_all(ysend, yret, s_y, r_y, edge, n)

        @apart
        def _():
            over(lead + 1, n, lag_step)
            over(lead, n, fold)

        def send_lags(d, _):
            q = d + (d >= me).astype(jnp.int32)
            send_lag(q, s_l, s_lo)
            return 0

        if unrolled:
            for d in range(lead, n - 1):
                send_lags(d, 0)
        else:
            lax.fori_loop(lead, n - 1, send_lags, 0)
        pltpu.make_async_copy(lsend.at[me], lret.at[where], r_l).start()
        remote(lsend.at[me], lret.at[where], s_lo, r_l, {"ch": mate}).start()

    if edge:
        @pl.when(is_edge)
        def _():
            size = per * rows
            hpad[...] = jnp.zeros(hpad.shape, f32)
            mlag[:, edge * block : (edge + 1) * block] = jnp.zeros((block, block), f32)
            drain(nv, r_nv)
            drain(nd, r_nd)

            @apart
            def _():
                for k in range(edge):
                    mlag[:, k * block : (k + 1) * block] = lax.dot_general(
                        flat(nv, 0, edge - k), flat(nd, k, edge), TN, preferred_element_type=f32
                    )
                over(0, edge, fold)

            buddy = first + place + high.astype(jnp.int32) * edge
            remote(lsend.at[:edge], few_lags, s_nl, r_nl, {"ctx": buddy}).start()
            drain(taps_few, r_nt)
            build(taps_few, edge)

            def near_products(src, shift_in, shift_out):
                for k in range(edge):
                    term = jnp.dot(
                        flat(src, k * shift_in, edge - k + k * shift_in), table(k, edge), preferred_element_type=f32
                    )
                    where = pl.ds(k * shift_out * size, (edge - k) * size)
                    if k == 0:
                        acc[where] = term
                    else:
                        acc[where] += term

            @apart
            def _():
                near_products(nv, 0, 1)
                nysend[...] = acc[: edge * size].astype(bf16).reshape(nysend.shape)

            among(lambda p: nysend.at[p], nyret, s_y, r_ny)

            @apart
            def _():
                near_products(nd, 1, 0)
                nbsend[...] = acc[: edge * size].astype(bf16).reshape(nbsend.shape)

            among(lambda p: nbsend.at[p], nbret, s_b, r_nb)

    def put_signal(*parts):
        joined = sum(part[...].reshape(width, block).astype(f32) for part in parts)
        gs_ref[...] = joined.T.astype(bf16)

    def put_gating(*parts):
        recomputed = sum(
            lax.dot_general(flip[...], part[...].reshape(width, block), NT, preferred_element_type=f32)
            for part in parts
        )
        gg_ref[...] = (cot_ref[...].astype(f32) * recomputed).astype(bf16)

    def put_taps(*parts):
        gt_ref[...] = sum(jnp.sum(part[...], axis=0) for part in parts) * norm

    @pl.when(jnp.logical_and(me >= edge, me < n - edge))
    def _():
        drain(bret, r_b)
        put_signal(bret)
        drain(yret, r_y)
        put_gating(yret)
        drain(lret, r_l)
        put_taps(lret)

    if edge:
        @pl.when(low)
        def _():
            drain(nyret, r_ny)
            put_gating(nyret)
            drain(nbret, r_nb)
            drain(bret, r_b)
            put_signal(nbret, bret)
            drain(lret, r_l)
            put_taps(lret)

        @pl.when(high)
        def _():
            drain(nbret, r_nb)
            put_signal(nbret)
            drain(nyret, r_ny)
            drain(yret, r_y)
            put_gating(nyret, yret)
            drain(lret, r_l)
            put_taps(lret)

    @pl.when(is_worker)
    def _():
        drain(taps_all.at[: workers - 1], s_t)
        drain(gsend.at[: workers - 1], s_g)
        drain(vsend.at[: workers - 1], s_v)
        if edge:
            pl.when(far)(lambda: drain(taps_all.at[:edge], s_nt))
        drain(bsend.at[: n - edge - 1], s_b)
        drain(lsend.at[:lead], s_l0)
        drain(lsend.at[:lead], s_lo0)
        drain(lsend.at[: n - lead - 1], s_l)
        drain(lsend.at[: n - lead], s_lo)
        drain(ysend.at[: n - edge - 1], s_y)

    @pl.when(is_edge)
    def _():
        drain(taps_all.at[:workers], s_t)
        if edge:
            pl.when(high)(lambda: drain(gsend, s_g))
            pl.when(low)(lambda: drain(vsend, s_v))
            drain(nv.at[: edge - 1], s_nv)
            drain(nd.at[: edge - 1], s_nd)
            drain(nysend.at[: edge - 1], s_y)
            drain(nbsend.at[: edge - 1], s_b)
            pl.when(low)(lambda: drain(taps_few.at[: edge - 1], s_nt))
            drain(lsend.at[:edge], s_nl)
        else:
            drain(gsend, s_g)
            drain(vsend, s_v)


def store(gs_in, gg_in, gt_in, gs_out, gg_out, gt_out, sems):
    copies = [
        pltpu.make_async_copy(src, dst, sems.at[i])
        for i, (src, dst) in enumerate(((gs_in, gs_out), (gg_in, gg_out), (gt_in, gt_out)))
    ]
    for copy in copies:
        copy.start()
    for copy in copies:
        copy.wait()


def body(signal, gating, filter_taps, cotangent):
    block, width = signal.shape
    n = lax.axis_size("ctx")
    pieces = lax.axis_size("ch")
    workers = WORKERS
    first = (n - workers) // 2
    rows = width // workers
    whole = n & (n - 1) == 0 and workers % 2 == 0 and first == workers // 2
    edge = first if whole else 0
    few = max(edge, 1)
    per = workers // few
    norm = 1.0 / math.sqrt(width * pieces * block * n)
    pad = 0 if n <= 16 else n
    hbm = pl.BlockSpec(memory_space=pltpu.HBM)
    vmem = pl.BlockSpec(memory_space=pltpu.VMEM)
    dma = pltpu.SemaphoreType.DMA
    results = (
        pltpu.VMEM((block, width), bf16),
        pltpu.VMEM((block, width), bf16),
        pltpu.VMEM((1, block), f32),
    )
    outputs = pl.pallas_call(
        functools.partial(kernel, n, workers, first, edge, norm),
        out_shape=results,
        in_specs=[hbm] * 4,
        out_specs=(vmem,) * 3,
        scratch_shapes=[
            pltpu.VMEM((block, width), bf16),
            pltpu.VMEM((block, width), bf16),
            pltpu.VMEM((block,), bf16),
            pltpu.VMEM((block, width), bf16),
            pltpu.VMEM((block, block), bf16),
            pltpu.VMEM((1, block), f32),
            pltpu.VMEM((workers, rows, block), bf16),
            pltpu.VMEM((workers, rows, block), bf16),
            pltpu.VMEM((n, 1, block), f32),
            pltpu.VMEM((n + pad, rows, block), bf16),
            pltpu.VMEM((n, rows, block), bf16),
            pltpu.VMEM((n, rows, block), bf16),
            pltpu.VMEM((n, rows, block), bf16),
            pltpu.VMEM((n, 1, block), f32),
            pltpu.VMEM((workers, rows, block), bf16),
            pltpu.VMEM((workers, rows, block), bf16),
            pltpu.VMEM((pieces * workers, 1, block), f32),
            pltpu.VMEM((1, (n + 1) * block + block // 2), f32),
            pltpu.VMEM((block // 2, (n + 1) * block), bf16),
            pltpu.VMEM(((n + pad) * rows, block), f32),
            pltpu.VMEM((block, (n + 1) * block), f32),
            pltpu.VMEM((few, 1, block), f32),
        ]
        + [pltpu.VMEM((few, per, rows, block), bf16)] * 6
        + [pltpu.VMEM((few, 1, block), f32)]
        + [dma] * 25
        + [dma((4,)), pltpu.SemaphoreType.REGULAR, pltpu.SemaphoreType.REGULAR],
        compiler_params=pltpu.CompilerParams(
            collective_id=0, has_side_effects=True, vmem_limit_bytes=60 * 1024 * 1024
        ),
    )(signal, gating, filter_taps, cotangent)
    outputs = [pltpu.with_memory_space_constraint(o, pltpu.VMEM) for o in outputs]
    grad_signal, grad_gating, grad_taps = pl.pallas_call(
        store,
        out_shape=(
            jax.ShapeDtypeStruct((block, width), bf16),
            jax.ShapeDtypeStruct((block, width), bf16),
            jax.ShapeDtypeStruct((1, block), f32),
        ),
        in_specs=[vmem] * 3,
        out_specs=(hbm,) * 3,
        scratch_shapes=[dma((3,))],
    )(*outputs)
    return (grad_signal, grad_gating, grad_taps.reshape(block))


def solution(mesh):
    in_specs = (P("ctx", "ch"), P("ctx", "ch"), P("ctx"), P("ctx", "ch"))
    out_specs = (P("ctx", "ch"), P("ctx", "ch"), P("ctx"))
    return jax.shard_map(body, mesh=mesh, in_specs=in_specs, out_specs=out_specs, check_vma=False)
```

```python
import functools
import math

import jax
import jax.numpy as jnp
from jax import lax
from jax.experimental import pallas as pl
from jax.experimental.pallas import tpu as pltpu
from jax.sharding import PartitionSpec as P

WORKERS = 8
ORDER = (3, 1, 2, 0)
OUT = (7, 11, 5, 9, 6, 10, 4, 8, 15, 3, 13, 1, 14, 2, 12)
SOON = (7, 11, 5, 9, 6, 10, 4, 8, 3, 1, 2)
LATER = (15, 13, 14, 12)
f32 = jnp.float32
bf16 = jnp.bfloat16
NT = (((1,), (1,)), ((), ()))
TN = (((0,), (0,)), ((), ()))


def kernel(
    n, workers, first, edge, norm,
    signal_hbm, gating_hbm, taps_hbm, cot_hbm,
    gs_ref, gg_ref, gt_ref,
    signal_ref, gating_ref, taps_ref, cot_ref, flip,
    tsend, gsend, vsend, taps_all, gpad, vpad,
    ysend, bsend, lsend, yret, bret, lret,
    hpad, toep, acc, mlag,
    taps_few, nv, nd, nysend, nbsend, nyret, nbret, nlret,
    s_t, s_g, s_v, s_y, s_b, s_l0, s_lo0, s_l, s_lo, s_nt, s_nv, s_nd,
    r_t, r_g, r_v, r_y, r_b, r_l, r_nt, r_nv, r_nd, r_ny, r_nb, r_nl,
    s_in, mate_in, heard,
):
    block, width = signal_ref.shape
    half = block // 2
    rows = width // workers
    total = n * rows
    unrolled = n <= 16
    me = lax.axis_index("ctx")
    ch = lax.axis_index("ch")
    mate = 1 - ch
    slot = me - first
    is_worker = jnp.logical_and(me >= first, me < first + workers)
    is_edge = jnp.logical_not(is_worker)
    low = me < edge
    high = me >= n - edge
    lead = max(edge, 1)

    barrier = pltpu.get_barrier_semaphore()

    near = is_worker & (slot < workers // 2)
    far = is_worker & (slot >= workers // 2)

    def greet(core):
        for d in range(1, n):
            pl.semaphore_signal(barrier, inc=1, device_id={"ctx": lax.rem(me + d, n), "ch": core})
        pl.when(ch != core)(lambda: pl.semaphore_signal(barrier, inc=1, device_id={"ch": core}))

    bits = [(1 - 2 * (me // 2**i % 2)) * 2**i for i in range((n - 1).bit_length())]

    def other(step):
        if n & (n - 1):
            return lax.rem(me + step, n)
        where = me
        for i, bit in enumerate(bits):
            where = where + (step // 2**i % 2) * bit
        return where

    pl.semaphore_signal(barrier, inc=1, device_id={"ch": mate})
    if edge:
        @pl.when(is_edge)
        def _():
            for i in range(1, edge):
                pl.semaphore_signal(barrier, inc=1, device_id={"ctx": other(i), "ch": 0})

        @pl.when(low)
        def _():
            for i in range(edge):
                pl.semaphore_signal(barrier, inc=1, device_id={"ctx": n - edge + i, "ch": 0})

    pl.when(near)(lambda: greet(0))
    pl.when(far)(lambda: greet(1))

    fetches = [
        pltpu.make_async_copy(src, dst, s_in.at[i])
        for i, (src, dst) in enumerate(
            ((taps_hbm, taps_ref), (cot_hbm, cot_ref), (gating_hbm, gating_ref), (signal_hbm, signal_ref))
        )
    ]
    for fetch in fetches:
        fetch.start()

    def remote(src, dst, send, recv, where):
        return pltpu.make_async_remote_copy(src_ref=src, dst_ref=dst, send_sem=send, recv_sem=recv, device_id=where)

    def drain(ref, sem):
        pltpu.make_async_copy(ref, ref, sem).wait()

    def to_workers(base, src, dst, send, recv):
        for i in ORDER:
            p = base + lax.rem(other(i), workers // 2)
            copy = remote(src(p), dst.at[me], send, recv, {"ctx": first + p})

            @pl.when(p != slot)
            def _():
                copy.start()

            @pl.when(p == slot)
            def _():
                pltpu.make_async_copy(src(p), dst.at[me], recv).start()

    def send_group(base):
        to_workers(base, lambda p: tsend, taps_all, s_t, r_t)

        @pl.when(me >= edge)
        def _():
            to_workers(base, lambda p: gsend.at[p], gpad, s_g, r_g)

        if edge:
            @pl.when(low)
            def _():
                to_workers(base, lambda p: vsend.at[p], vpad, s_v, r_v)

    def send_late(base):
        to_workers(base, lambda p: vsend.at[p], vpad, s_v, r_v)

    across = lax.broadcasted_iota(jnp.int32, (block, block), 0)
    along = lax.broadcasted_iota(jnp.int32, (block, block), 1)
    flip[...] = jnp.where(across + along == block - 1, 1.0, 0.0).astype(bf16)

    fetches[0].wait()
    own_taps = jnp.broadcast_to(taps_ref[...].astype(f32).reshape(1, block), (16, block)).astype(bf16)
    tsend[...] = jnp.dot(own_taps, flip[...], preferred_element_type=f32)[:1]
    fetches[1].wait()
    fetches[2].wait()
    grad_mid = (cot_ref[...].astype(f32) * gating_ref[...].astype(f32)).astype(bf16)
    gsend[...] = grad_mid.astype(f32).T.astype(bf16).reshape(workers, rows, block)
    fetches[3].wait()
    vsend[...] = (
        lax.dot_general(signal_ref[...], flip[...], TN, preferred_element_type=f32)
        .astype(bf16)
        .reshape(workers, rows, block)
    )

    def entered(core, group):
        @pl.when(ch == core)
        def _():
            extra = 0
            if edge and core == 0:
                extra = is_edge.astype(jnp.int32) * 2 * (edge - 1) + high.astype(jnp.int32) * 2 * edge
            pl.semaphore_wait(barrier, workers + 1 - group.astype(jnp.int32) + extra)
            pl.semaphore_signal(heard, inc=1, device_id={"ch": mate})

        @pl.when(ch != core)
        def _():
            pl.semaphore_wait(heard, 1)

    entered(0, near)
    send_group(0)
    if edge:
        per = workers // edge
        base = me - me % edge
        place = me % edge

        def among(src, dst, send, recv):
            for i in range(1, edge):
                q = other(i)
                remote(src(q - base), dst.at[place], send, recv, {"ctx": q}).start()
            pltpu.make_async_copy(src(place), dst.at[place], recv).start()

        @pl.when(is_edge)
        def _():
            pl.when(low)(lambda: among(lambda p: tsend, taps_few, s_nt, r_nt))
            among(lambda p: vsend.at[pl.ds(p * per, per)], nv, s_nv, r_nv)
            among(lambda p: gsend.at[pl.ds(p * per, per)], nd, s_nd, r_nd)

    entered(1, far)
    send_group(workers // 2)

    @pl.when(jnp.logical_and(me >= edge, me < n - edge))
    def _():
        send_late(0)
        send_late(workers // 2)

    def at(k, size):
        return k * size if isinstance(k, int) else pl.multiple_of(k * size, half)

    def build(taps, m):
        for j in range(m):
            start = half + (m - 1 - j) * block
            hpad[:, start : start + block] = taps[j]
        for j in range(m + 1):
            window = jnp.broadcast_to(hpad[:, j * block : (j + 1) * block + half], (half, block + half))
            turned = pltpu.roll(window, 1, 1, stride=1, stride_axis=0)
            toep[:, j * block : (j + 1) * block] = turned[:, half:].astype(bf16)

    def table(k, m=n):
        start = at(m - k, block)
        upper = toep[:, pl.ds(start, block)]
        lower = toep[:, pl.ds(start - half if isinstance(k, int) else pl.multiple_of(start - half, half), block)]
        return jnp.concatenate([upper, lower], axis=0)

    def over(low_k, high_k, step):
        if unrolled:
            for k in range(low_k, high_k):
                step(k)
        else:
            lax.fori_loop(low_k, high_k, lambda k, _: (step(k), 0)[1], 0)

    def span_of(k):
        return max(0, edge - k), min(n - edge, n - k)

    def flat(ref, start, stop):
        part = ref[start:stop]
        return part.reshape(-1, block)

    def products(src, shift_in, shift_out):
        for k in [edge] + [k for k in range(n) if k != edge]:
            start, stop = span_of(k)
            term = jnp.dot(
                flat(src, start + k * shift_in, stop + k * shift_in), table(k), preferred_element_type=f32
            )
            where = pl.ds((start + k * shift_out) * rows, (stop - start) * rows)
            if k == edge:
                acc[where] = term
            else:
                acc[where] += term

    def backward_step(k):
        acc[:total] += jnp.dot(
            gpad[pl.ds(k, n)].reshape(total, block), table(k), preferred_element_type=f32
        )

    def forward_step(k):
        start = pl.multiple_of(k * rows, 16)
        acc[pl.ds(start, total)] += jnp.dot(
            vpad[...].reshape(total, block), table(k), preferred_element_type=f32
        )

    def lag_step(k):
        if unrolled:
            start, stop = span_of(k)
            left, right = flat(vpad, start, stop), flat(gpad, start + k, stop + k)
        else:
            left, right = vpad[...].reshape(total, block), gpad[pl.ds(k, n)].reshape(total, block)
        mlag[:, pl.ds(at(k, block), block)] = lax.dot_general(left, right, TN, preferred_element_type=f32)

    def fold(k):
        span = block + half
        start = at(k, block)
        later = start + half if unrolled else pl.multiple_of(start + half, half)
        part = mlag[:half, pl.ds(later, span)] + mlag[half:, pl.ds(start, span)]
        turned = pltpu.roll(part, 1, 1, stride=1, stride_axis=0)[:, half:]
        lsend[pl.ds(k, 1)] = jnp.sum(turned, axis=0, keepdims=True)[None]

    def to_all(src, dst, send, recv, start, stop, steps=OUT):
        def step(d, _):
            q = other(d)
            copy = remote(src.at[q], dst.at[slot], send, recv, {"ctx": q})
            if start == 0 and stop == n:
                copy.start()
            else:
                pl.when(jnp.logical_and(q >= start, q < stop))(copy.start)
            return 0

        if n == 16:
            for d in steps:
                step(d, 0)
        else:
            lax.fori_loop(1, n, step, 0)
        if steps is not LATER:
            pltpu.make_async_copy(src.at[me], dst.at[slot], recv).start()

    apart = pl.when(me >= 0)

    @pl.when(is_worker)
    def _():
        if not unrolled:
            gpad[n:] = jnp.zeros((n, rows, block), bf16)
        hpad[...] = jnp.zeros(hpad.shape, f32)
        mlag[:, n * block :] = jnp.zeros((block, block), f32)
        drain(taps_all, r_t)
        if edge:
            onward = remote(taps_all.at[:edge], taps_few, s_nt, r_nt, {"ctx": slot + n - workers})
            pl.when(far)(onward.start)
        build(taps_all, n)
        drain(gpad.at[edge:n], r_g)
        pl.semaphore_signal(mate_in, inc=1, device_id={"ch": mate})

        @apart
        def _():
            if unrolled:
                products(gpad, 1, 0)
            else:
                acc[...] = jnp.zeros(acc.shape, f32)
                over(0, n, backward_step)
            bsend[: n - edge] = acc[: (n - edge) * rows].astype(bf16).reshape(n - edge, rows, block)

        to_all(bsend, bret, s_b, r_b, 0, n - edge, SOON if n == 16 else OUT)

        drain(vpad.at[: n - edge], r_v)

        @apart
        def _():
            over(0, lead + 1, lag_step)
            over(0, lead, fold)

        where = ch * workers + slot

        def send_lag(q, own, across):
            remote(lsend.at[q], lret.at[where], own, r_l, {"ctx": q}).start()
            remote(lsend.at[q], lret.at[where], across, r_l, {"ctx": q, "ch": mate}).start()

        pl.semaphore_wait(mate_in, 1)
        for q in range(lead):
            send_lag(q, s_l0, s_lo0)
        if n == 16:
            to_all(bsend, bret, s_b, r_b, 0, n - edge, LATER)

        @apart
        def _():
            if unrolled:
                products(vpad, 0, 1)
            else:
                acc[...] = jnp.zeros(acc.shape, f32)
                over(0, n, forward_step)
            ysend[edge:] = acc[edge * rows : total].astype(bf16).reshape(n - edge, rows, block)

        to_all(ysend, yret, s_y, r_y, edge, n)

        @apart
        def _():
            over(lead + 1, n, lag_step)
            over(lead, n, fold)

        def send_lags(d, _):
            q = d + (d >= me).astype(jnp.int32)
            send_lag(q, s_l, s_lo)
            return 0

        if unrolled:
            for d in range(lead, n - 1):
                send_lags(d, 0)
        else:
            lax.fori_loop(lead, n - 1, send_lags, 0)
        pltpu.make_async_copy(lsend.at[me], lret.at[where], r_l).start()
        remote(lsend.at[me], lret.at[where], s_lo, r_l, {"ch": mate}).start()

    if edge:
        @pl.when(is_edge)
        def _():
            size = per * rows
            hpad[...] = jnp.zeros(hpad.shape, f32)
            mlag[:, edge * block : (edge + 1) * block] = jnp.zeros((block, block), f32)
            def near_products(src, shift_in, shift_out):
                for k in range(edge):
                    term = jnp.dot(
                        flat(src, k * shift_in, edge - k + k * shift_in), table(k, edge), preferred_element_type=f32
                    )
                    where = pl.ds(k * shift_out * size, (edge - k) * size)
                    if k == 0:
                        acc[where] = term
                    else:
                        acc[where] += term

            def near_forward():
                drain(taps_few, r_nt)
                build(taps_few, edge)

                @apart
                def _():
                    near_products(nv, 0, 1)
                    nysend[...] = acc[: edge * size].astype(bf16).reshape(nysend.shape)

                among(lambda p: nysend.at[p], nyret, s_y, r_ny)

            drain(nv, r_nv)
            pl.when(low)(near_forward)
            drain(nd, r_nd)

            @apart
            def _():
                for k in range(edge):
                    mlag[:, k * block : (k + 1) * block] = lax.dot_general(
                        flat(nv, 0, edge - k), flat(nd, k, edge), TN, preferred_element_type=f32
                    )
                over(0, edge, fold)

            row = (ch * 2 + high.astype(jnp.int32)) * edge + place
            for q in range(edge):
                pl.when(me != q)(remote(lsend.at[q], nlret.at[row], s_l, r_nl, {"ctx": q}).start)
                remote(lsend.at[q], nlret.at[row], s_lo, r_nl, {"ctx": q, "ch": mate}).start()

            @pl.when(low)
            def _():
                pltpu.make_async_copy(lsend.at[me], nlret.at[row], r_nl).start()

            pl.when(high)(near_forward)

            @apart
            def _():
                near_products(nd, 1, 0)
                nbsend[...] = acc[: edge * size].astype(bf16).reshape(nbsend.shape)

            among(lambda p: nbsend.at[p], nbret, s_b, r_nb)

    def put_signal(*parts):
        joined = sum(part[...].reshape(width, block).astype(f32) for part in parts)
        gs_ref[...] = joined.T.astype(bf16)

    def put_gating(*parts):
        recomputed = sum(
            lax.dot_general(flip[...], part[...].reshape(width, block), NT, preferred_element_type=f32)
            for part in parts
        )
        gg_ref[...] = (cot_ref[...].astype(f32) * recomputed).astype(bf16)

    def put_taps(*parts):
        gt_ref[...] = sum(jnp.sum(part[...], axis=0) for part in parts) * norm

    @pl.when(jnp.logical_and(me >= edge, me < n - edge))
    def _():
        drain(bret, r_b)
        put_signal(bret)
        drain(yret, r_y)
        put_gating(yret)
        drain(lret, r_l)
        put_taps(lret)

    if edge:
        @pl.when(low)
        def _():
            drain(nyret, r_ny)
            put_gating(nyret)
            drain(nbret, r_nb)
            drain(bret, r_b)
            put_signal(nbret, bret)
            drain(nlret, r_nl)
            drain(lret, r_l)
            put_taps(nlret, lret)

        @pl.when(high)
        def _():
            drain(nbret, r_nb)
            put_signal(nbret)
            drain(nyret, r_ny)
            drain(yret, r_y)
            put_gating(nyret, yret)
            drain(lret, r_l)
            put_taps(lret)

    @pl.when(is_worker)
    def _():
        drain(taps_all.at[: workers - 1], s_t)
        drain(gsend.at[: workers - 1], s_g)
        drain(vsend.at[: workers - 1], s_v)
        if edge:
            pl.when(far)(lambda: drain(taps_all.at[:edge], s_nt))
        drain(bsend.at[: n - edge - 1], s_b)
        drain(lsend.at[:lead], s_l0)
        drain(lsend.at[:lead], s_lo0)
        drain(lsend.at[: n - lead - 1], s_l)
        drain(lsend.at[: n - lead], s_lo)
        drain(ysend.at[: n - edge - 1], s_y)

    @pl.when(is_edge)
    def _():
        drain(taps_all.at[:workers], s_t)
        if edge:
            pl.when(high)(lambda: drain(gsend, s_g))
            pl.when(low)(lambda: drain(vsend, s_v))
            drain(nv.at[: edge - 1], s_nv)
            drain(nd.at[: edge - 1], s_nd)
            drain(nysend.at[: edge - 1], s_y)
            drain(nbsend.at[: edge - 1], s_b)
            pl.when(low)(lambda: drain(taps_few.at[: edge - 1], s_nt))
            pl.when(low)(lambda: drain(lsend.at[: edge - 1], s_l))
            pl.when(high)(lambda: drain(lsend.at[:edge], s_l))
            drain(lsend.at[:edge], s_lo)
        else:
            drain(gsend, s_g)
            drain(vsend, s_v)


def store(gs_in, gg_in, gt_in, gs_out, gg_out, gt_out, sems):
    copies = [
        pltpu.make_async_copy(src, dst, sems.at[i])
        for i, (src, dst) in enumerate(((gs_in, gs_out), (gg_in, gg_out), (gt_in, gt_out)))
    ]
    for copy in copies:
        copy.start()
    for copy in copies:
        copy.wait()


def body(signal, gating, filter_taps, cotangent):
    block, width = signal.shape
    n = lax.axis_size("ctx")
    pieces = lax.axis_size("ch")
    workers = WORKERS
    first = (n - workers) // 2
    rows = width // workers
    whole = n & (n - 1) == 0 and workers % 2 == 0 and first == workers // 2
    edge = first if whole else 0
    few = max(edge, 1)
    per = workers // few
    norm = 1.0 / math.sqrt(width * pieces * block * n)
    pad = 0 if n <= 16 else n
    hbm = pl.BlockSpec(memory_space=pltpu.HBM)
    vmem = pl.BlockSpec(memory_space=pltpu.VMEM)
    dma = pltpu.SemaphoreType.DMA
    results = (
        pltpu.VMEM((block, width), bf16),
        pltpu.VMEM((block, width), bf16),
        pltpu.VMEM((1, block), f32),
    )
    outputs = pl.pallas_call(
        functools.partial(kernel, n, workers, first, edge, norm),
        out_shape=results,
        in_specs=[hbm] * 4,
        out_specs=(vmem,) * 3,
        scratch_shapes=[
            pltpu.VMEM((block, width), bf16),
            pltpu.VMEM((block, width), bf16),
            pltpu.VMEM((block,), bf16),
            pltpu.VMEM((block, width), bf16),
            pltpu.VMEM((block, block), bf16),
            pltpu.VMEM((1, block), f32),
            pltpu.VMEM((workers, rows, block), bf16),
            pltpu.VMEM((workers, rows, block), bf16),
            pltpu.VMEM((n, 1, block), f32),
            pltpu.VMEM((n + pad, rows, block), bf16),
            pltpu.VMEM((n, rows, block), bf16),
            pltpu.VMEM((n, rows, block), bf16),
            pltpu.VMEM((n, rows, block), bf16),
            pltpu.VMEM((n, 1, block), f32),
            pltpu.VMEM((workers, rows, block), bf16),
            pltpu.VMEM((workers, rows, block), bf16),
            pltpu.VMEM((pieces * workers, 1, block), f32),
            pltpu.VMEM((1, (n + 1) * block + block // 2), f32),
            pltpu.VMEM((block // 2, (n + 1) * block), bf16),
            pltpu.VMEM(((n + pad) * rows, block), f32),
            pltpu.VMEM((block, (n + 1) * block), f32),
            pltpu.VMEM((few, 1, block), f32),
        ]
        + [pltpu.VMEM((few, per, rows, block), bf16)] * 6
        + [pltpu.VMEM((2 * pieces * few, 1, block), f32)]
        + [dma] * 24
        + [dma((4,)), pltpu.SemaphoreType.REGULAR, pltpu.SemaphoreType.REGULAR],
        compiler_params=pltpu.CompilerParams(
            collective_id=0, has_side_effects=True, vmem_limit_bytes=60 * 1024 * 1024
        ),
    )(signal, gating, filter_taps, cotangent)
    outputs = [pltpu.with_memory_space_constraint(o, pltpu.VMEM) for o in outputs]
    grad_signal, grad_gating, grad_taps = pl.pallas_call(
        store,
        out_shape=(
            jax.ShapeDtypeStruct((block, width), bf16),
            jax.ShapeDtypeStruct((block, width), bf16),
            jax.ShapeDtypeStruct((1, block), f32),
        ),
        in_specs=[vmem] * 3,
        out_specs=(hbm,) * 3,
        scratch_shapes=[dma((3,))],
    )(*outputs)
    return (grad_signal, grad_gating, grad_taps.reshape(block))


def solution(mesh):
    in_specs = (P("ctx", "ch"), P("ctx", "ch"), P("ctx"), P("ctx", "ch"))
    out_specs = (P("ctx", "ch"), P("ctx", "ch"), P("ctx"))
    return jax.shard_map(body, mesh=mesh, in_specs=in_specs, out_specs=out_specs, check_vma=False)
```

```python
import functools
import math

import jax
import jax.numpy as jnp
from jax import lax
from jax.experimental import pallas as pl
from jax.experimental.pallas import tpu as pltpu
from jax.sharding import PartitionSpec as P

WORKERS = 8
ORDER = (3, 1, 2, 0)
OUT = (7, 11, 5, 9, 6, 10, 4, 8, 15, 3, 13, 1, 14, 2, 12)
f32 = jnp.float32
bf16 = jnp.bfloat16
NT = (((1,), (1,)), ((), ()))
TN = (((0,), (0,)), ((), ()))


def kernel(
    n, workers, first, edge, norm,
    signal_hbm, gating_hbm, taps_hbm, cot_hbm,
    gs_ref, gg_ref, gt_ref,
    signal_ref, gating_ref, taps_ref, cot_ref, flip,
    tsend, gsend, vsend, taps_all, gpad, vpad,
    ysend, bsend, lsend, yret, bret, lret,
    hpad, toep, acc, mlag,
    taps_few, nv, nd, nysend, nbsend, nyret, nbret, nlret,
    s_t, s_g, s_v, s_y, s_b, s_l0, s_lo0, s_l, s_lo, s_nt, s_nv, s_nd,
    r_t, r_g, r_v, r_y, r_b, r_l, r_nt, r_nv, r_nd, r_ny, r_nb, r_nl,
    s_in, mate_in, heard,
):
    block, width = signal_ref.shape
    half = block // 2
    rows = width // workers
    total = n * rows
    unrolled = n <= 16
    me = lax.axis_index("ctx")
    ch = lax.axis_index("ch")
    mate = 1 - ch
    slot = me - first
    is_worker = jnp.logical_and(me >= first, me < first + workers)
    is_edge = jnp.logical_not(is_worker)
    low = me < edge
    high = me >= n - edge
    lead = max(edge, 1)

    barrier = pltpu.get_barrier_semaphore()

    near = is_worker & (slot < workers // 2)
    far = is_worker & (slot >= workers // 2)

    def greet(core):
        for d in range(1, n):
            pl.semaphore_signal(barrier, inc=1, device_id={"ctx": lax.rem(me + d, n), "ch": core})
        pl.when(ch != core)(lambda: pl.semaphore_signal(barrier, inc=1, device_id={"ch": core}))

    bits = [(1 - 2 * (me // 2**i % 2)) * 2**i for i in range((n - 1).bit_length())]

    def other(step):
        if n & (n - 1):
            return lax.rem(me + step, n)
        where = me
        for i, bit in enumerate(bits):
            where = where + (step // 2**i % 2) * bit
        return where

    pl.semaphore_signal(barrier, inc=1, device_id={"ch": mate})
    if edge:
        @pl.when(is_edge)
        def _():
            for i in range(1, edge):
                pl.semaphore_signal(barrier, inc=1, device_id={"ctx": other(i), "ch": 0})

        @pl.when(low)
        def _():
            for i in range(edge):
                pl.semaphore_signal(barrier, inc=1, device_id={"ctx": n - edge + i, "ch": 0})

    pl.when(near)(lambda: greet(0))
    pl.when(far)(lambda: greet(1))

    fetches = [
        pltpu.make_async_copy(src, dst, s_in.at[i])
        for i, (src, dst) in enumerate(
            ((taps_hbm, taps_ref), (cot_hbm, cot_ref), (gating_hbm, gating_ref), (signal_hbm, signal_ref))
        )
    ]
    for fetch in fetches:
        fetch.start()

    def remote(src, dst, send, recv, where):
        return pltpu.make_async_remote_copy(src_ref=src, dst_ref=dst, send_sem=send, recv_sem=recv, device_id=where)

    def drain(ref, sem):
        pltpu.make_async_copy(ref, ref, sem).wait()

    def to_workers(base, src, dst, send, recv):
        for i in ORDER:
            p = base + lax.rem(other(i), workers // 2)
            copy = remote(src(p), dst.at[me], send, recv, {"ctx": first + p})

            @pl.when(p != slot)
            def _():
                copy.start()

            @pl.when(p == slot)
            def _():
                pltpu.make_async_copy(src(p), dst.at[me], recv).start()

    def send_group(base):
        @pl.when(me >= edge)
        def _():
            to_workers(base, lambda p: gsend.at[p], gpad, s_g, r_g)

        if edge:
            @pl.when(low)
            def _():
                to_workers(base, lambda p: vsend.at[p], vpad, s_v, r_v)

    def send_late(base):
        to_workers(base, lambda p: vsend.at[p], vpad, s_v, r_v)

    across = lax.broadcasted_iota(jnp.int32, (block, block), 0)
    along = lax.broadcasted_iota(jnp.int32, (block, block), 1)
    flip[...] = jnp.where(across + along == block - 1, 1.0, 0.0).astype(bf16)

    fetches[0].wait()
    own_taps = jnp.broadcast_to(taps_ref[...].astype(f32).reshape(1, block), (16, block)).astype(bf16)
    tsend[...] = jnp.dot(own_taps, flip[...], preferred_element_type=f32)[:1]
    fetches[1].wait()
    fetches[2].wait()
    grad_mid = (cot_ref[...].astype(f32) * gating_ref[...].astype(f32)).astype(bf16)
    gsend[...] = grad_mid.astype(f32).T.astype(bf16).reshape(workers, rows, block)
    fetches[3].wait()
    vsend[...] = (
        lax.dot_general(signal_ref[...], flip[...], TN, preferred_element_type=f32)
        .astype(bf16)
        .reshape(workers, rows, block)
    )

    def entered(core, group):
        @pl.when(ch == core)
        def _():
            extra = 0
            if edge and core == 0:
                extra = is_edge.astype(jnp.int32) * 2 * (edge - 1) + high.astype(jnp.int32) * 2 * edge
            pl.semaphore_wait(barrier, workers + 1 - group.astype(jnp.int32) + extra)
            pl.semaphore_signal(heard, inc=1, device_id={"ch": mate})

        @pl.when(ch != core)
        def _():
            pl.semaphore_wait(heard, 1)

    entered(0, near)
    to_workers(0, lambda p: tsend, taps_all, s_t, r_t)
    if edge:
        per = workers // edge
        base = me - me % edge
        place = me % edge

        def among(src, dst, send, recv):
            for i in range(1, edge):
                q = other(i)
                remote(src(q - base), dst.at[place], send, recv, {"ctx": q}).start()
            pltpu.make_async_copy(src(place), dst.at[place], recv).start()

        @pl.when(is_edge)
        def _():
            pl.when(low)(lambda: among(lambda p: tsend, taps_few, s_nt, r_nt))
            among(lambda p: vsend.at[pl.ds(p * per, per)], nv, s_nv, r_nv)
            among(lambda p: gsend.at[pl.ds(p * per, per)], nd, s_nd, r_nd)

    entered(1, far)
    to_workers(workers // 2, lambda p: tsend, taps_all, s_t, r_t)
    send_group(0)
    send_group(workers // 2)

    @pl.when(jnp.logical_and(me >= edge, me < n - edge))
    def _():
        send_late(0)
        send_late(workers // 2)

    def at(k, size):
        return k * size if isinstance(k, int) else pl.multiple_of(k * size, half)

    def build(taps, m):
        for j in range(m):
            start = half + (m - 1 - j) * block
            hpad[:, start : start + block] = taps[j]
        for j in range(m + 1):
            window = jnp.broadcast_to(hpad[:, j * block : (j + 1) * block + half], (half, block + half))
            turned = pltpu.roll(window, 1, 1, stride=1, stride_axis=0)
            toep[:, j * block : (j + 1) * block] = turned[:, half:].astype(bf16)

    def table(k, m=n):
        start = at(m - k, block)
        upper = toep[:, pl.ds(start, block)]
        lower = toep[:, pl.ds(start - half if isinstance(k, int) else pl.multiple_of(start - half, half), block)]
        return jnp.concatenate([upper, lower], axis=0)

    def over(low_k, high_k, step):
        if unrolled:
            for k in range(low_k, high_k):
                step(k)
        else:
            lax.fori_loop(low_k, high_k, lambda k, _: (step(k), 0)[1], 0)

    def span_of(k):
        return max(0, edge - k), min(n - edge, n - k)

    def flat(ref, start, stop):
        part = ref[start:stop]
        return part.reshape(-1, block)

    def products(src, shift_in, shift_out):
        for k in [edge] + [k for k in range(n) if k != edge]:
            start, stop = span_of(k)
            term = jnp.dot(
                flat(src, start + k * shift_in, stop + k * shift_in), table(k), preferred_element_type=f32
            )
            where = pl.ds((start + k * shift_out) * rows, (stop - start) * rows)
            if k == edge:
                acc[where] = term
            else:
                acc[where] += term

    def backward_step(k):
        acc[:total] += jnp.dot(
            gpad[pl.ds(k, n)].reshape(total, block), table(k), preferred_element_type=f32
        )

    def forward_step(k):
        start = pl.multiple_of(k * rows, 16)
        acc[pl.ds(start, total)] += jnp.dot(
            vpad[...].reshape(total, block), table(k), preferred_element_type=f32
        )

    def lag_step(k):
        if unrolled:
            start, stop = span_of(k)
            left, right = flat(vpad, start, stop), flat(gpad, start + k, stop + k)
        else:
            left, right = vpad[...].reshape(total, block), gpad[pl.ds(k, n)].reshape(total, block)
        mlag[:, pl.ds(at(k, block), block)] = lax.dot_general(left, right, TN, preferred_element_type=f32)

    def fold(k):
        span = block + half
        start = at(k, block)
        later = start + half if unrolled else pl.multiple_of(start + half, half)
        part = mlag[:half, pl.ds(later, span)] + mlag[half:, pl.ds(start, span)]
        turned = pltpu.roll(part, 1, 1, stride=1, stride_axis=0)[:, half:]
        lsend[pl.ds(k, 1)] = jnp.sum(turned, axis=0, keepdims=True)[None]

    def to_all(src, dst, send, recv, start, stop, steps=OUT):
        def step(d, _):
            q = other(d)
            copy = remote(src.at[q], dst.at[slot], send, recv, {"ctx": q})
            if start == 0 and stop == n:
                copy.start()
            else:
                pl.when(jnp.logical_and(q >= start, q < stop))(copy.start)
            return 0

        if n == 16:
            for d in steps:
                step(d, 0)
        else:
            lax.fori_loop(1, n, step, 0)
        pltpu.make_async_copy(src.at[me], dst.at[slot], recv).start()

    apart = pl.when(me >= 0)

    @pl.when(is_worker)
    def _():
        if not unrolled:
            gpad[n:] = jnp.zeros((n, rows, block), bf16)
        hpad[...] = jnp.zeros(hpad.shape, f32)
        mlag[:, n * block :] = jnp.zeros((block, block), f32)
        drain(taps_all, r_t)
        if edge:
            onward = remote(taps_all.at[:edge], taps_few, s_nt, r_nt, {"ctx": slot + n - workers})
            pl.when(far)(onward.start)
        build(taps_all, n)
        drain(gpad.at[edge:n], r_g)
        pl.semaphore_signal(mate_in, inc=1, device_id={"ch": mate})

        @apart
        def _():
            if unrolled:
                products(gpad, 1, 0)
            else:
                acc[...] = jnp.zeros(acc.shape, f32)
                over(0, n, backward_step)
            bsend[: n - edge] = acc[: (n - edge) * rows].astype(bf16).reshape(n - edge, rows, block)

        remote(bsend.at[0], bret.at[slot], s_b, r_b, {"ctx": 0}).start()
        for d in (3, 1, 2):
            q = other(d)
            remote(bsend.at[q], bret.at[slot], s_b, r_b, {"ctx": q}).start()

        drain(vpad.at[: n - edge], r_v)

        @apart
        def _():
            over(0, lead + 1, lag_step)
            over(0, lead, fold)

        where = ch * workers + slot

        def send_lag(q, own, across):
            remote(lsend.at[q], lret.at[where], own, r_l, {"ctx": q}).start()
            remote(lsend.at[q], lret.at[where], across, r_l, {"ctx": q, "ch": mate}).start()

        pl.semaphore_wait(mate_in, 1)
        for q in range(lead):
            send_lag(q, s_l0, s_lo0)
        to_all(bsend, bret, s_b, r_b, 1, n - edge, (7, 11, 5, 9, 6, 10, 4, 8, 15, 13, 14, 12))

        @apart
        def _():
            if unrolled:
                products(vpad, 0, 1)
            else:
                acc[...] = jnp.zeros(acc.shape, f32)
                over(0, n, forward_step)
            ysend[edge:] = acc[edge * rows : total].astype(bf16).reshape(n - edge, rows, block)

        to_all(ysend, yret, s_y, r_y, edge, n)

        @apart
        def _():
            over(lead + 1, n, lag_step)
            over(lead, n, fold)

        def send_lags(d, _):
            q = d + (d >= me).astype(jnp.int32)
            send_lag(q, s_l, s_lo)
            return 0

        if unrolled:
            for d in range(lead, n - 1):
                send_lags(d, 0)
        else:
            lax.fori_loop(lead, n - 1, send_lags, 0)
        pltpu.make_async_copy(lsend.at[me], lret.at[where], r_l).start()
        remote(lsend.at[me], lret.at[where], s_lo, r_l, {"ch": mate}).start()

    if edge:
        @pl.when(is_edge)
        def _():
            size = per * rows
            hpad[...] = jnp.zeros(hpad.shape, f32)
            mlag[:, edge * block : (edge + 1) * block] = jnp.zeros((block, block), f32)
            def near_products(src, shift_in, shift_out):
                for k in range(edge):
                    term = jnp.dot(
                        flat(src, k * shift_in, edge - k + k * shift_in), table(k, edge), preferred_element_type=f32
                    )
                    where = pl.ds(k * shift_out * size, (edge - k) * size)
                    if k == 0:
                        acc[where] = term
                    else:
                        acc[where] += term

            def near_forward():
                drain(taps_few, r_nt)
                build(taps_few, edge)

                @apart
                def _():
                    near_products(nv, 0, 1)
                    nysend[...] = acc[: edge * size].astype(bf16).reshape(nysend.shape)

                among(lambda p: nysend.at[p], nyret, s_y, r_ny)

            drain(nv, r_nv)
            pl.when(low)(near_forward)
            drain(nd, r_nd)

            @apart
            def _():
                for k in range(edge):
                    mlag[:, k * block : (k + 1) * block] = lax.dot_general(
                        flat(nv, 0, edge - k), flat(nd, k, edge), TN, preferred_element_type=f32
                    )
                over(0, edge, fold)

            row = (ch * 2 + high.astype(jnp.int32)) * edge + place
            for q in range(edge):
                pl.when(me != q)(remote(lsend.at[q], nlret.at[row], s_l, r_nl, {"ctx": q}).start)
                remote(lsend.at[q], nlret.at[row], s_lo, r_nl, {"ctx": q, "ch": mate}).start()

            @pl.when(low)
            def _():
                pltpu.make_async_copy(lsend.at[me], nlret.at[row], r_nl).start()

            pl.when(high)(near_forward)

            @apart
            def _():
                near_products(nd, 1, 0)
                nbsend[...] = acc[: edge * size].astype(bf16).reshape(nbsend.shape)

            among(lambda p: nbsend.at[p], nbret, s_b, r_nb)

    def put_signal(*parts):
        joined = sum(part[...].reshape(width, block).astype(f32) for part in parts)
        gs_ref[...] = joined.T.astype(bf16)

    def put_gating(*parts):
        recomputed = sum(
            lax.dot_general(flip[...], part[...].reshape(width, block), NT, preferred_element_type=f32)
            for part in parts
        )
        gg_ref[...] = (cot_ref[...].astype(f32) * recomputed).astype(bf16)

    def put_taps(*parts):
        gt_ref[...] = sum(jnp.sum(part[...], axis=0) for part in parts) * norm

    @pl.when(jnp.logical_and(me >= edge, me < n - edge))
    def _():
        drain(bret, r_b)
        put_signal(bret)
        drain(yret, r_y)
        put_gating(yret)
        drain(lret, r_l)
        put_taps(lret)

    if edge:
        @pl.when(low)
        def _():
            drain(nyret, r_ny)
            put_gating(nyret)
            drain(nbret, r_nb)
            drain(bret, r_b)
            put_signal(nbret, bret)
            drain(nlret, r_nl)
            drain(lret, r_l)
            put_taps(nlret, lret)

        @pl.when(high)
        def _():
            drain(nbret, r_nb)
            put_signal(nbret)
            drain(nyret, r_ny)
            drain(yret, r_y)
            put_gating(nyret, yret)
            drain(lret, r_l)
            put_taps(lret)

    @pl.when(is_worker)
    def _():
        drain(taps_all.at[: workers - 1], s_t)
        drain(gsend.at[: workers - 1], s_g)
        drain(vsend.at[: workers - 1], s_v)
        if edge:
            pl.when(far)(lambda: drain(taps_all.at[:edge], s_nt))
        drain(bsend.at[: n - edge - 1], s_b)
        drain(lsend.at[:lead], s_l0)
        drain(lsend.at[:lead], s_lo0)
        drain(lsend.at[: n - lead - 1], s_l)
        drain(lsend.at[: n - lead], s_lo)
        drain(ysend.at[: n - edge - 1], s_y)

    @pl.when(is_edge)
    def _():
        drain(taps_all.at[:workers], s_t)
        if edge:
            pl.when(high)(lambda: drain(gsend, s_g))
            pl.when(low)(lambda: drain(vsend, s_v))
            drain(nv.at[: edge - 1], s_nv)
            drain(nd.at[: edge - 1], s_nd)
            drain(nysend.at[: edge - 1], s_y)
            drain(nbsend.at[: edge - 1], s_b)
            pl.when(low)(lambda: drain(taps_few.at[: edge - 1], s_nt))
            pl.when(low)(lambda: drain(lsend.at[: edge - 1], s_l))
            pl.when(high)(lambda: drain(lsend.at[:edge], s_l))
            drain(lsend.at[:edge], s_lo)
        else:
            drain(gsend, s_g)
            drain(vsend, s_v)


def store(gs_in, gg_in, gt_in, gs_out, gg_out, gt_out, sems):
    copies = [
        pltpu.make_async_copy(src, dst, sems.at[i])
        for i, (src, dst) in enumerate(((gs_in, gs_out), (gg_in, gg_out), (gt_in, gt_out)))
    ]
    for copy in copies:
        copy.start()
    for copy in copies:
        copy.wait()


def body(signal, gating, filter_taps, cotangent):
    block, width = signal.shape
    n = lax.axis_size("ctx")
    pieces = lax.axis_size("ch")
    workers = WORKERS
    first = (n - workers) // 2
    rows = width // workers
    whole = n & (n - 1) == 0 and workers % 2 == 0 and first == workers // 2
    edge = first if whole else 0
    few = max(edge, 1)
    per = workers // few
    norm = 1.0 / math.sqrt(width * pieces * block * n)
    pad = 0 if n <= 16 else n
    hbm = pl.BlockSpec(memory_space=pltpu.HBM)
    vmem = pl.BlockSpec(memory_space=pltpu.VMEM)
    dma = pltpu.SemaphoreType.DMA
    results = (
        pltpu.VMEM((block, width), bf16),
        pltpu.VMEM((block, width), bf16),
        pltpu.VMEM((1, block), f32),
    )
    outputs = pl.pallas_call(
        functools.partial(kernel, n, workers, first, edge, norm),
        out_shape=results,
        in_specs=[hbm] * 4,
        out_specs=(vmem,) * 3,
        scratch_shapes=[
            pltpu.VMEM((block, width), bf16),
            pltpu.VMEM((block, width), bf16),
            pltpu.VMEM((block,), bf16),
            pltpu.VMEM((block, width), bf16),
            pltpu.VMEM((block, block), bf16),
            pltpu.VMEM((1, block), f32),
            pltpu.VMEM((workers, rows, block), bf16),
            pltpu.VMEM((workers, rows, block), bf16),
            pltpu.VMEM((n, 1, block), f32),
            pltpu.VMEM((n + pad, rows, block), bf16),
            pltpu.VMEM((n, rows, block), bf16),
            pltpu.VMEM((n, rows, block), bf16),
            pltpu.VMEM((n, rows, block), bf16),
            pltpu.VMEM((n, 1, block), f32),
            pltpu.VMEM((workers, rows, block), bf16),
            pltpu.VMEM((workers, rows, block), bf16),
            pltpu.VMEM((pieces * workers, 1, block), f32),
            pltpu.VMEM((1, (n + 1) * block + block // 2), f32),
            pltpu.VMEM((block // 2, (n + 1) * block), bf16),
            pltpu.VMEM(((n + pad) * rows, block), f32),
            pltpu.VMEM((block, (n + 1) * block), f32),
            pltpu.VMEM((few, 1, block), f32),
        ]
        + [pltpu.VMEM((few, per, rows, block), bf16)] * 6
        + [pltpu.VMEM((2 * pieces * few, 1, block), f32)]
        + [dma] * 24
        + [dma((4,)), pltpu.SemaphoreType.REGULAR, pltpu.SemaphoreType.REGULAR],
        compiler_params=pltpu.CompilerParams(
            collective_id=0, has_side_effects=True, vmem_limit_bytes=60 * 1024 * 1024
        ),
    )(signal, gating, filter_taps, cotangent)
    outputs = [pltpu.with_memory_space_constraint(o, pltpu.VMEM) for o in outputs]
    grad_signal, grad_gating, grad_taps = pl.pallas_call(
        store,
        out_shape=(
            jax.ShapeDtypeStruct((block, width), bf16),
            jax.ShapeDtypeStruct((block, width), bf16),
            jax.ShapeDtypeStruct((1, block), f32),
        ),
        in_specs=[vmem] * 3,
        out_specs=(hbm,) * 3,
        scratch_shapes=[dma((3,))],
    )(*outputs)
    return (grad_signal, grad_gating, grad_taps.reshape(block))


def solution(mesh):
    in_specs = (P("ctx", "ch"), P("ctx", "ch"), P("ctx"), P("ctx", "ch"))
    out_specs = (P("ctx", "ch"), P("ctx", "ch"), P("ctx"))
    return jax.shard_map(body, mesh=mesh, in_specs=in_specs, out_specs=out_specs, check_vma=False)
```

```python
import functools
import math

import jax
import jax.numpy as jnp
from jax import lax
from jax.experimental import pallas as pl
from jax.experimental.pallas import tpu as pltpu
from jax.sharding import PartitionSpec as P

WORKERS = 8
ORDER = (3, 1, 2, 0)
OUT = (7, 11, 5, 9, 6, 10, 4, 8, 15, 3, 13, 1, 14, 2, 12)
f32 = jnp.float32
bf16 = jnp.bfloat16
NT = (((1,), (1,)), ((), ()))
TN = (((0,), (0,)), ((), ()))


def kernel(
    n, workers, first, edge, norm,
    signal_hbm, gating_hbm, taps_hbm, cot_hbm,
    gs_ref, gg_ref, gt_ref,
    signal_ref, gating_ref, taps_ref, cot_ref, flip,
    tsend, gsend, vsend, taps_all, gpad, vpad,
    ysend, bsend, lsend, yret, bret, lret,
    hpad, toep, acc, mlag,
    taps_few, nv, nd, nysend, nbsend, nyret, nbret, nlret,
    s_t, s_g, s_v, s_y, s_b, s_l0, s_lo0, s_l, s_lo, s_nt, s_nv, s_nd,
    r_t, r_g, r_v, r_y, r_b, r_l, r_nt, r_nv, r_nd, r_ny, r_nb, r_nl,
    s_in, mate_in, heard,
):
    block, width = signal_ref.shape
    half = block // 2
    rows = width // workers
    total = n * rows
    unrolled = n <= 16
    me = lax.axis_index("ctx")
    ch = lax.axis_index("ch")
    mate = 1 - ch
    slot = me - first
    is_worker = jnp.logical_and(me >= first, me < first + workers)
    is_edge = jnp.logical_not(is_worker)
    low = me < edge
    high = me >= n - edge
    lead = max(edge, 1)

    barrier = pltpu.get_barrier_semaphore()

    near = is_worker & (slot < workers // 2)
    far = is_worker & (slot >= workers // 2)

    def greet(core):
        for d in range(1, n):
            pl.semaphore_signal(barrier, inc=1, device_id={"ctx": lax.rem(me + d, n), "ch": core})
        pl.when(ch != core)(lambda: pl.semaphore_signal(barrier, inc=1, device_id={"ch": core}))

    bits = [(1 - 2 * (me // 2**i % 2)) * 2**i for i in range((n - 1).bit_length())]

    def other(step):
        if n & (n - 1):
            return lax.rem(me + step, n)
        where = me
        for i, bit in enumerate(bits):
            where = where + (step // 2**i % 2) * bit
        return where

    pl.semaphore_signal(barrier, inc=1, device_id={"ch": mate})
    if edge:
        @pl.when(is_edge)
        def _():
            for i in range(1, edge):
                pl.semaphore_signal(barrier, inc=1, device_id={"ctx": other(i), "ch": 0})

        @pl.when(low)
        def _():
            for i in range(edge):
                pl.semaphore_signal(barrier, inc=1, device_id={"ctx": n - edge + i, "ch": 0})

    pl.when(near)(lambda: greet(0))
    pl.when(far)(lambda: greet(1))

    fetches = [
        pltpu.make_async_copy(src, dst, s_in.at[i])
        for i, (src, dst) in enumerate(
            ((taps_hbm, taps_ref), (cot_hbm, cot_ref), (gating_hbm, gating_ref), (signal_hbm, signal_ref))
        )
    ]
    for fetch in fetches:
        fetch.start()

    def remote(src, dst, send, recv, where):
        return pltpu.make_async_remote_copy(src_ref=src, dst_ref=dst, send_sem=send, recv_sem=recv, device_id=where)

    def drain(ref, sem):
        pltpu.make_async_copy(ref, ref, sem).wait()

    def to_workers(bases, src, dst, send, recv):
        for i in ORDER:
            for base in bases:
                p = base + lax.rem(other(i), workers // 2)
                copy = remote(src(p), dst.at[me], send, recv, {"ctx": first + p})

                @pl.when(p != slot)
                def _():
                    copy.start()

                @pl.when(p == slot)
                def _():
                    pltpu.make_async_copy(src(p), dst.at[me], recv).start()

    both = (0, workers // 2) if 'r' not in "i" else (workers // 2, 0)

    def send_group():
        @pl.when(me >= edge)
        def _():
            to_workers(both, lambda p: gsend.at[p], gpad, s_g, r_g)

        if edge:
            @pl.when(low)
            def _():
                to_workers(both, lambda p: vsend.at[p], vpad, s_v, r_v)

    def send_late():
        to_workers(both, lambda p: vsend.at[p], vpad, s_v, r_v)

    across = lax.broadcasted_iota(jnp.int32, (block, block), 0)
    along = lax.broadcasted_iota(jnp.int32, (block, block), 1)
    flip[...] = jnp.where(across + along == block - 1, 1.0, 0.0).astype(bf16)

    fetches[0].wait()
    own_taps = jnp.broadcast_to(taps_ref[...].astype(f32).reshape(1, block), (16, block)).astype(bf16)
    tsend[...] = jnp.dot(own_taps, flip[...], preferred_element_type=f32)[:1]
    fetches[1].wait()
    fetches[2].wait()
    grad_mid = (cot_ref[...].astype(f32) * gating_ref[...].astype(f32)).astype(bf16)
    gsend[...] = grad_mid.astype(f32).T.astype(bf16).reshape(workers, rows, block)
    fetches[3].wait()
    vsend[...] = (
        lax.dot_general(signal_ref[...], flip[...], TN, preferred_element_type=f32)
        .astype(bf16)
        .reshape(workers, rows, block)
    )

    def entered(core, group):
        @pl.when(ch == core)
        def _():
            extra = 0
            if edge and core == 0:
                extra = is_edge.astype(jnp.int32) * 2 * (edge - 1) + high.astype(jnp.int32) * 2 * edge
            pl.semaphore_wait(barrier, workers + 1 - group.astype(jnp.int32) + extra)
            pl.semaphore_signal(heard, inc=1, device_id={"ch": mate})

        @pl.when(ch != core)
        def _():
            pl.semaphore_wait(heard, 1)

    entered(0, near)
    to_workers((0,), lambda p: tsend, taps_all, s_t, r_t)
    if edge:
        per = workers // edge
        base = me - me % edge
        place = me % edge

        def among(src, dst, send, recv):
            for i in range(1, edge):
                q = other(i)
                remote(src(q - base), dst.at[place], send, recv, {"ctx": q}).start()
            pltpu.make_async_copy(src(place), dst.at[place], recv).start()

        @pl.when(is_edge)
        def _():
            pl.when(low)(lambda: among(lambda p: tsend, taps_few, s_nt, r_nt))
            among(lambda p: vsend.at[pl.ds(p * per, per)], nv, s_nv, r_nv)
            among(lambda p: gsend.at[pl.ds(p * per, per)], nd, s_nd, r_nd)

    entered(1, far)
    to_workers((workers // 2,), lambda p: tsend, taps_all, s_t, r_t)
    send_group()

    @pl.when(jnp.logical_and(me >= edge, me < n - edge))
    def _():
        send_late()

    def at(k, size):
        return k * size if isinstance(k, int) else pl.multiple_of(k * size, half)

    def build(taps, m):
        for j in range(m):
            start = half + (m - 1 - j) * block
            hpad[:, start : start + block] = taps[j]
        for j in range(m + 1):
            window = jnp.broadcast_to(hpad[:, j * block : (j + 1) * block + half], (half, block + half))
            turned = pltpu.roll(window, 1, 1, stride=1, stride_axis=0)
            toep[:, j * block : (j + 1) * block] = turned[:, half:].astype(bf16)

    def table(k, m=n):
        start = at(m - k, block)
        upper = toep[:, pl.ds(start, block)]
        lower = toep[:, pl.ds(start - half if isinstance(k, int) else pl.multiple_of(start - half, half), block)]
        return jnp.concatenate([upper, lower], axis=0)

    def over(low_k, high_k, step):
        if unrolled:
            for k in range(low_k, high_k):
                step(k)
        else:
            lax.fori_loop(low_k, high_k, lambda k, _: (step(k), 0)[1], 0)

    def span_of(k):
        return max(0, edge - k), min(n - edge, n - k)

    def flat(ref, start, stop):
        part = ref[start:stop]
        return part.reshape(-1, block)

    def products(src, shift_in, shift_out):
        for k in [edge] + [k for k in range(n) if k != edge]:
            start, stop = span_of(k)
            term = jnp.dot(
                flat(src, start + k * shift_in, stop + k * shift_in), table(k), preferred_element_type=f32
            )
            where = pl.ds((start + k * shift_out) * rows, (stop - start) * rows)
            if k == edge:
                acc[where] = term
            else:
                acc[where] += term

    def backward_step(k):
        acc[:total] += jnp.dot(
            gpad[pl.ds(k, n)].reshape(total, block), table(k), preferred_element_type=f32
        )

    def forward_step(k):
        start = pl.multiple_of(k * rows, 16)
        acc[pl.ds(start, total)] += jnp.dot(
            vpad[...].reshape(total, block), table(k), preferred_element_type=f32
        )

    def lag_step(k):
        if unrolled:
            start, stop = span_of(k)
            left, right = flat(vpad, start, stop), flat(gpad, start + k, stop + k)
        else:
            left, right = vpad[...].reshape(total, block), gpad[pl.ds(k, n)].reshape(total, block)
        mlag[:, pl.ds(at(k, block), block)] = lax.dot_general(left, right, TN, preferred_element_type=f32)

    def fold(k, count=1):
        span = count * block + half
        start = at(k, block)
        later = start + half if unrolled else pl.multiple_of(start + half, half)
        part = mlag[:half, pl.ds(later, span)] + mlag[half:, pl.ds(start, span)]
        turned = pltpu.roll(part, 1, 1, stride=1, stride_axis=0)[:, half:]
        row = jnp.sum(turned, axis=0, keepdims=True)
        for i in range(count):
            lsend[pl.ds(k + i, 1)] = row[:, i * block : (i + 1) * block][None]

    def to_all(src, dst, send, recv, start, stop, steps=OUT):
        def step(d, _):
            q = other(d)
            copy = remote(src.at[q], dst.at[slot], send, recv, {"ctx": q})
            if start == 0 and stop == n:
                copy.start()
            else:
                pl.when(jnp.logical_and(q >= start, q < stop))(copy.start)
            return 0

        if n == 16:
            for d in steps:
                step(d, 0)
        else:
            lax.fori_loop(1, n, step, 0)
        pltpu.make_async_copy(src.at[me], dst.at[slot], recv).start()

    apart = pl.when(me >= 0)

    @pl.when(is_worker)
    def _():
        if not unrolled:
            gpad[n:] = jnp.zeros((n, rows, block), bf16)
        hpad[...] = jnp.zeros(hpad.shape, f32)
        mlag[:, n * block :] = jnp.zeros((block, block), f32)
        drain(taps_all, r_t)
        if edge:
            onward = remote(taps_all.at[:edge], taps_few, s_nt, r_nt, {"ctx": slot + n - workers})
            pl.when(far)(onward.start)
        build(taps_all, n)
        drain(gpad.at[edge:n], r_g)
        pl.semaphore_signal(mate_in, inc=1, device_id={"ch": mate})

        @apart
        def _():
            if unrolled:
                products(gpad, 1, 0)
            else:
                acc[...] = jnp.zeros(acc.shape, f32)
                over(0, n, backward_step)
            bsend[: n - edge] = acc[: (n - edge) * rows].astype(bf16).reshape(n - edge, rows, block)

        remote(bsend.at[0], bret.at[slot], s_b, r_b, {"ctx": 0}).start()
        for d in (3, 1, 2) if n == 16 else ():
            q = other(d)
            remote(bsend.at[q], bret.at[slot], s_b, r_b, {"ctx": q}).start()

        drain(vpad.at[: n - edge], r_v)

        @apart
        def _():
            over(0, lead + 1, lag_step)
            if unrolled:
                for k in range(0, lead, 2):
                    fold(k, min(2, lead - k))
            else:
                over(0, lead, fold)

        where = ch * workers + slot

        def send_lag(q, own, across):
            remote(lsend.at[q], lret.at[where], own, r_l, {"ctx": q}).start()
            remote(lsend.at[q], lret.at[where], across, r_l, {"ctx": q, "ch": mate}).start()

        pl.semaphore_wait(mate_in, 1)
        for q in range(lead):
            send_lag(q, s_l0, s_lo0)
        to_all(bsend, bret, s_b, r_b, 1, n - edge, (7, 11, 5, 9, 6, 10, 4, 8, 15, 13, 14, 12))

        @apart
        def _():
            if unrolled:
                products(vpad, 0, 1)
            else:
                acc[...] = jnp.zeros(acc.shape, f32)
                over(0, n, forward_step)
            ysend[edge:] = acc[edge * rows : total].astype(bf16).reshape(n - edge, rows, block)

        to_all(ysend, yret, s_y, r_y, edge, n)

        @apart
        def _():
            over(lead + 1, n, lag_step)
            if unrolled:
                for k in range(lead, n, 2):
                    fold(k, min(2, n - k))
            else:
                over(lead, n, fold)

        def send_lags(d, _):
            q = d + (d >= me).astype(jnp.int32)
            send_lag(q, s_l, s_lo)
            return 0

        if unrolled:
            for d in range(lead, n - 1):
                send_lags(d, 0)
        else:
            lax.fori_loop(lead, n - 1, send_lags, 0)
        pltpu.make_async_copy(lsend.at[me], lret.at[where], r_l).start()
        remote(lsend.at[me], lret.at[where], s_lo, r_l, {"ch": mate}).start()

    if edge:
        @pl.when(is_edge)
        def _():
            size = per * rows
            hpad[...] = jnp.zeros(hpad.shape, f32)
            mlag[:, edge * block : (edge + 1) * block] = jnp.zeros((block, block), f32)
            def near_products(src, shift_in, shift_out):
                for k in range(edge):
                    term = jnp.dot(
                        flat(src, k * shift_in, edge - k + k * shift_in), table(k, edge), preferred_element_type=f32
                    )
                    where = pl.ds(k * shift_out * size, (edge - k) * size)
                    if k == 0:
                        acc[where] = term
                    else:
                        acc[where] += term

            def near_forward():
                drain(taps_few, r_nt)
                build(taps_few, edge)

                @apart
                def _():
                    near_products(nv, 0, 1)
                    nysend[...] = acc[: edge * size].astype(bf16).reshape(nysend.shape)

                among(lambda p: nysend.at[p], nyret, s_y, r_ny)

            drain(nv, r_nv)
            pl.when(low)(near_forward)
            drain(nd, r_nd)

            @apart
            def _():
                for k in range(edge):
                    mlag[:, k * block : (k + 1) * block] = lax.dot_general(
                        flat(nv, 0, edge - k), flat(nd, k, edge), TN, preferred_element_type=f32
                    )
                over(0, edge, fold)

            row = (ch * 2 + high.astype(jnp.int32)) * edge + place
            for q in range(edge):
                pl.when(me != q)(remote(lsend.at[q], nlret.at[row], s_l, r_nl, {"ctx": q}).start)
                remote(lsend.at[q], nlret.at[row], s_lo, r_nl, {"ctx": q, "ch": mate}).start()

            @pl.when(low)
            def _():
                pltpu.make_async_copy(lsend.at[me], nlret.at[row], r_nl).start()

            pl.when(high)(near_forward)

            @apart
            def _():
                near_products(nd, 1, 0)
                nbsend[...] = acc[: edge * size].astype(bf16).reshape(nbsend.shape)

            among(lambda p: nbsend.at[p], nbret, s_b, r_nb)

    def put_signal(*parts):
        joined = sum(part[...].reshape(width, block).astype(f32) for part in parts)
        gs_ref[...] = joined.T.astype(bf16)

    def put_gating(*parts):
        recomputed = sum(
            lax.dot_general(flip[...], part[...].reshape(width, block), NT, preferred_element_type=f32)
            for part in parts
        )
        gg_ref[...] = (cot_ref[...].astype(f32) * recomputed).astype(bf16)

    def put_taps(*parts):
        gt_ref[...] = sum(jnp.sum(part[...], axis=0) for part in parts) * norm

    @pl.when(jnp.logical_and(me >= edge, me < n - edge))
    def _():
        drain(bret, r_b)
        put_signal(bret)
        drain(yret, r_y)
        put_gating(yret)
        drain(lret, r_l)
        put_taps(lret)

    if edge:
        @pl.when(low)
        def _():
            drain(nyret, r_ny)
            put_gating(nyret)
            drain(nbret, r_nb)
            drain(bret, r_b)
            put_signal(nbret, bret)
            drain(nlret, r_nl)
            drain(lret, r_l)
            put_taps(nlret, lret)

        @pl.when(high)
        def _():
            drain(nbret, r_nb)
            put_signal(nbret)
            drain(nyret, r_ny)
            drain(yret, r_y)
            put_gating(nyret, yret)
            drain(lret, r_l)
            put_taps(lret)

    @pl.when(is_worker)
    def _():
        drain(taps_all.at[: workers - 1], s_t)
        drain(gsend.at[: workers - 1], s_g)
        drain(vsend.at[: workers - 1], s_v)
        if edge:
            pl.when(far)(lambda: drain(taps_all.at[:edge], s_nt))
        drain(bsend.at[: n - edge - 1], s_b)
        drain(lsend.at[:lead], s_l0)
        drain(lsend.at[:lead], s_lo0)
        drain(lsend.at[: n - lead - 1], s_l)
        drain(lsend.at[: n - lead], s_lo)
        drain(ysend.at[: n - edge - 1], s_y)

    @pl.when(is_edge)
    def _():
        drain(taps_all.at[:workers], s_t)
        if edge:
            pl.when(high)(lambda: drain(gsend, s_g))
            pl.when(low)(lambda: drain(vsend, s_v))
            drain(nv.at[: edge - 1], s_nv)
            drain(nd.at[: edge - 1], s_nd)
            drain(nysend.at[: edge - 1], s_y)
            drain(nbsend.at[: edge - 1], s_b)
            pl.when(low)(lambda: drain(taps_few.at[: edge - 1], s_nt))
            pl.when(low)(lambda: drain(lsend.at[: edge - 1], s_l))
            pl.when(high)(lambda: drain(lsend.at[:edge], s_l))
            drain(lsend.at[:edge], s_lo)
        else:
            drain(gsend, s_g)
            drain(vsend, s_v)


def store(gs_in, gg_in, gt_in, gs_out, gg_out, gt_out, sems):
    copies = [
        pltpu.make_async_copy(src, dst, sems.at[i])
        for i, (src, dst) in enumerate(((gs_in, gs_out), (gg_in, gg_out), (gt_in, gt_out)))
    ]
    for copy in copies:
        copy.start()
    for copy in copies:
        copy.wait()


def body(signal, gating, filter_taps, cotangent):
    block, width = signal.shape
    n = lax.axis_size("ctx")
    pieces = lax.axis_size("ch")
    workers = WORKERS
    first = (n - workers) // 2
    rows = width // workers
    whole = n & (n - 1) == 0 and workers % 2 == 0 and first == workers // 2
    edge = first if whole else 0
    few = max(edge, 1)
    per = workers // few
    norm = 1.0 / math.sqrt(width * pieces * block * n)
    pad = 0 if n <= 16 else n
    hbm = pl.BlockSpec(memory_space=pltpu.HBM)
    vmem = pl.BlockSpec(memory_space=pltpu.VMEM)
    dma = pltpu.SemaphoreType.DMA
    results = (
        pltpu.VMEM((block, width), bf16),
        pltpu.VMEM((block, width), bf16),
        pltpu.VMEM((1, block), f32),
    )
    outputs = pl.pallas_call(
        functools.partial(kernel, n, workers, first, edge, norm),
        out_shape=results,
        in_specs=[hbm] * 4,
        out_specs=(vmem,) * 3,
        scratch_shapes=[
            pltpu.VMEM((block, width), bf16),
            pltpu.VMEM((block, width), bf16),
            pltpu.VMEM((block,), bf16),
            pltpu.VMEM((block, width), bf16),
            pltpu.VMEM((block, block), bf16),
            pltpu.VMEM((1, block), f32),
            pltpu.VMEM((workers, rows, block), bf16),
            pltpu.VMEM((workers, rows, block), bf16),
            pltpu.VMEM((n, 1, block), f32),
            pltpu.VMEM((n + pad, rows, block), bf16),
            pltpu.VMEM((n, rows, block), bf16),
            pltpu.VMEM((n, rows, block), bf16),
            pltpu.VMEM((n, rows, block), bf16),
            pltpu.VMEM((n, 1, block), f32),
            pltpu.VMEM((workers, rows, block), bf16),
            pltpu.VMEM((workers, rows, block), bf16),
            pltpu.VMEM((pieces * workers, 1, block), f32),
            pltpu.VMEM((1, (n + 1) * block + block // 2), f32),
            pltpu.VMEM((block // 2, (n + 1) * block), bf16),
            pltpu.VMEM(((n + pad) * rows, block), f32),
            pltpu.VMEM((block, (n + 1) * block), f32),
            pltpu.VMEM((few, 1, block), f32),
        ]
        + [pltpu.VMEM((few, per, rows, block), bf16)] * 6
        + [pltpu.VMEM((2 * pieces * few, 1, block), f32)]
        + [dma] * 24
        + [dma((4,)), pltpu.SemaphoreType.REGULAR, pltpu.SemaphoreType.REGULAR],
        compiler_params=pltpu.CompilerParams(
            collective_id=0, has_side_effects=True, vmem_limit_bytes=60 * 1024 * 1024
        ),
    )(signal, gating, filter_taps, cotangent)
    outputs = [pltpu.with_memory_space_constraint(o, pltpu.VMEM) for o in outputs]
    grad_signal, grad_gating, grad_taps = pl.pallas_call(
        store,
        out_shape=(
            jax.ShapeDtypeStruct((block, width), bf16),
            jax.ShapeDtypeStruct((block, width), bf16),
            jax.ShapeDtypeStruct((1, block), f32),
        ),
        in_specs=[vmem] * 3,
        out_specs=(hbm,) * 3,
        scratch_shapes=[dma((3,))],
    )(*outputs)
    return (grad_signal, grad_gating, grad_taps.reshape(block))


def solution(mesh):
    in_specs = (P("ctx", "ch"), P("ctx", "ch"), P("ctx"), P("ctx", "ch"))
    out_specs = (P("ctx", "ch"), P("ctx", "ch"), P("ctx"))
    return jax.shard_map(body, mesh=mesh, in_specs=in_specs, out_specs=out_specs, check_vma=False)
```

```python
import functools
import math

import jax
import jax.numpy as jnp
from jax import lax
from jax.experimental import pallas as pl
from jax.experimental.pallas import tpu as pltpu
from jax.sharding import PartitionSpec as P

WORKERS = 8
ORDER = (3, 1, 2, 0)
OUT = (7, 11, 5, 9, 6, 10, 4, 8, 15, 3, 13, 1, 14, 2, 12)
f32 = jnp.float32
bf16 = jnp.bfloat16
NT = (((1,), (1,)), ((), ()))
TN = (((0,), (0,)), ((), ()))


def kernel(
    n, workers, first, edge, norm,
    signal_hbm, gating_hbm, taps_hbm, cot_hbm,
    gs_ref, gg_ref, gt_ref,
    signal_ref, gating_ref, taps_ref, cot_ref, flip,
    tsend, gsend, vsend, taps_all, gpad, vpad,
    ysend, bsend, lsend, yret, bret, lret,
    hpad, toep, acc, mlag,
    taps_few, nv, nd, nysend, nbsend, nyret, nbret, nlret,
    s_t, s_g, s_v, s_y, s_b, s_l0, s_lo0, s_l, s_lo, s_nt, s_nv, s_nd,
    r_t, r_g, r_v, r_y, r_b, r_l, r_nt, r_nv, r_nd, r_ny, r_nb, r_nl,
    s_in, mate_in, heard,
):
    block, width = signal_ref.shape
    half = block // 2
    rows = width // workers
    total = n * rows
    unrolled = n <= 16
    me = lax.axis_index("ctx")
    ch = lax.axis_index("ch")
    mate = 1 - ch
    slot = me - first
    is_worker = jnp.logical_and(me >= first, me < first + workers)
    is_edge = jnp.logical_not(is_worker)
    low = me < edge
    high = me >= n - edge
    lead = max(edge, 1)

    barrier = pltpu.get_barrier_semaphore()

    near = is_worker & (slot < workers // 2)
    far = is_worker & (slot >= workers // 2)

    def greet(core):
        for d in range(1, n):
            pl.semaphore_signal(barrier, inc=1, device_id={"ctx": lax.rem(me + d, n), "ch": core})
        pl.when(ch != core)(lambda: pl.semaphore_signal(barrier, inc=1, device_id={"ch": core}))

    bits = [(1 - 2 * (me // 2**i % 2)) * 2**i for i in range((n - 1).bit_length())]

    def other(step):
        if n & (n - 1):
            return lax.rem(me + step, n)
        where = me
        for i, bit in enumerate(bits):
            where = where + (step // 2**i % 2) * bit
        return where

    pl.semaphore_signal(barrier, inc=1, device_id={"ch": mate})
    if edge:
        @pl.when(is_edge)
        def _():
            for i in range(1, edge):
                pl.semaphore_signal(barrier, inc=1, device_id={"ctx": other(i), "ch": 0})

        @pl.when(low)
        def _():
            for i in range(edge):
                pl.semaphore_signal(barrier, inc=1, device_id={"ctx": n - edge + i, "ch": 0})

    pl.when(near)(lambda: greet(0))
    pl.when(far)(lambda: greet(1))

    fetches = [
        pltpu.make_async_copy(src, dst, s_in.at[i])
        for i, (src, dst) in enumerate(
            ((taps_hbm, taps_ref), (cot_hbm, cot_ref), (gating_hbm, gating_ref), (signal_hbm, signal_ref))
        )
    ]
    for fetch in fetches:
        fetch.start()

    def remote(src, dst, send, recv, where):
        return pltpu.make_async_remote_copy(src_ref=src, dst_ref=dst, send_sem=send, recv_sem=recv, device_id=where)

    def drain(ref, sem):
        pltpu.make_async_copy(ref, ref, sem).wait()

    def to_workers(bases, src, dst, send, recv):
        for i in ORDER:
            for base in bases:
                p = base + lax.rem(other(i), workers // 2)
                copy = remote(src(p), dst.at[me], send, recv, {"ctx": first + p})

                @pl.when(p != slot)
                def _():
                    copy.start()

                @pl.when(p == slot)
                def _():
                    pltpu.make_async_copy(src(p), dst.at[me], recv).start()

    both = (0, workers // 2) if 'r' not in "i" else (workers // 2, 0)

    def send_group():
        @pl.when(me >= edge)
        def _():
            to_workers(both, lambda p: gsend.at[p], gpad, s_g, r_g)

        if edge:
            @pl.when(low)
            def _():
                to_workers(both, lambda p: vsend.at[p], vpad, s_v, r_v)

    def send_late():
        to_workers(both, lambda p: vsend.at[p], vpad, s_v, r_v)

    across = lax.broadcasted_iota(jnp.int32, (block, block), 0)
    along = lax.broadcasted_iota(jnp.int32, (block, block), 1)
    flip[...] = jnp.where(across + along == block - 1, 1.0, 0.0).astype(bf16)

    fetches[0].wait()
    own_taps = jnp.broadcast_to(taps_ref[...].astype(f32).reshape(1, block), (16, block)).astype(bf16)
    tsend[...] = jnp.dot(own_taps, flip[...], preferred_element_type=f32)[:1]
    fetches[1].wait()
    fetches[2].wait()
    grad_mid = (cot_ref[...].astype(f32) * gating_ref[...].astype(f32)).astype(bf16)
    gsend[...] = grad_mid.astype(f32).T.astype(bf16).reshape(workers, rows, block)
    fetches[3].wait()
    vsend[...] = (
        lax.dot_general(signal_ref[...], flip[...], TN, preferred_element_type=f32)
        .astype(bf16)
        .reshape(workers, rows, block)
    )

    def entered(core, group):
        @pl.when(ch == core)
        def _():
            extra = 0
            if edge and core == 0:
                extra = is_edge.astype(jnp.int32) * 2 * (edge - 1) + high.astype(jnp.int32) * 2 * edge
            pl.semaphore_wait(barrier, workers + 1 - group.astype(jnp.int32) + extra)
            pl.semaphore_signal(heard, inc=1, device_id={"ch": mate})

        @pl.when(ch != core)
        def _():
            pl.semaphore_wait(heard, 1)

    entered(0, near)
    to_workers((0,), lambda p: tsend, taps_all, s_t, r_t)
    if edge:
        per = workers // edge
        base = me - me % edge
        place = me % edge

        def among(src, dst, send, recv):
            for i in range(1, edge):
                q = other(i)
                remote(src(q - base), dst.at[place], send, recv, {"ctx": q}).start()
            pltpu.make_async_copy(src(place), dst.at[place], recv).start()

        @pl.when(is_edge)
        def _():
            pl.when(low)(lambda: among(lambda p: tsend, taps_few, s_nt, r_nt))
            among(lambda p: vsend.at[pl.ds(p * per, per)], nv, s_nv, r_nv)
            among(lambda p: gsend.at[pl.ds(p * per, per)], nd, s_nd, r_nd)

    entered(1, far)
    to_workers((workers // 2,), lambda p: tsend, taps_all, s_t, r_t)
    send_group()

    @pl.when(jnp.logical_and(me >= edge, me < n - edge))
    def _():
        send_late()

    def at(k, size):
        return k * size if isinstance(k, int) else pl.multiple_of(k * size, half)

    def build(taps, m):
        for j in range(m):
            start = half + (m - 1 - j) * block
            hpad[:, start : start + block] = taps[j]
        for j in range(m + 1):
            window = jnp.broadcast_to(hpad[:, j * block : (j + 1) * block + half], (half, block + half))
            turned = pltpu.roll(window, 1, 1, stride=1, stride_axis=0)
            toep[:, j * block : (j + 1) * block] = turned[:, half:].astype(bf16)

    def table(k, m=n):
        start = at(m - k, block)
        upper = toep[:, pl.ds(start, block)]
        lower = toep[:, pl.ds(start - half if isinstance(k, int) else pl.multiple_of(start - half, half), block)]
        return jnp.concatenate([upper, lower], axis=0)

    def over(low_k, high_k, step):
        if unrolled:
            for k in range(low_k, high_k):
                step(k)
        else:
            lax.fori_loop(low_k, high_k, lambda k, _: (step(k), 0)[1], 0)

    def span_of(k):
        return max(0, edge - k), min(n - edge, n - k)

    def flat(ref, start, stop):
        part = ref[start:stop]
        return part.reshape(-1, block)

    def products(src, shift_in, shift_out):
        for k in [edge] + [k for k in range(n) if k != edge]:
            start, stop = span_of(k)
            term = jnp.dot(
                flat(src, start + k * shift_in, stop + k * shift_in), table(k), preferred_element_type=f32
            )
            where = pl.ds((start + k * shift_out) * rows, (stop - start) * rows)
            if k == edge:
                acc[where] = term
            else:
                acc[where] += term

    def backward_step(k):
        acc[:total] += jnp.dot(
            gpad[pl.ds(k, n)].reshape(total, block), table(k), preferred_element_type=f32
        )

    def forward_step(k):
        start = pl.multiple_of(k * rows, 16)
        acc[pl.ds(start, total)] += jnp.dot(
            vpad[...].reshape(total, block), table(k), preferred_element_type=f32
        )

    def lag_step(k):
        if unrolled:
            start, stop = span_of(k)
            left, right = flat(vpad, start, stop), flat(gpad, start + k, stop + k)
        else:
            left, right = vpad[...].reshape(total, block), gpad[pl.ds(k, n)].reshape(total, block)
        mlag[:, pl.ds(at(k, block), block)] = lax.dot_general(left, right, TN, preferred_element_type=f32)

    def fold(k, count=1):
        span = count * block + half
        start = at(k, block)
        later = start + half if unrolled else pl.multiple_of(start + half, half)
        part = mlag[:half, pl.ds(later, span)] + mlag[half:, pl.ds(start, span)]
        turned = pltpu.roll(part, 1, 1, stride=1, stride_axis=0)[:, half:]
        row = jnp.sum(turned, axis=0, keepdims=True)
        for i in range(count):
            lsend[pl.ds(k + i, 1)] = row[:, i * block : (i + 1) * block][None]

    def to_all(src, dst, send, recv, start, stop, steps=OUT):
        def step(d, _):
            q = other(d)
            copy = remote(src.at[q], dst.at[slot], send, recv, {"ctx": q})
            if start == 0 and stop == n:
                copy.start()
            else:
                pl.when(jnp.logical_and(q >= start, q < stop))(copy.start)
            return 0

        if n == 16:
            for d in steps:
                step(d, 0)
        else:
            lax.fori_loop(1, n, step, 0)
        pltpu.make_async_copy(src.at[me], dst.at[slot], recv).start()

    apart = pl.when(me >= 0)

    @pl.when(is_worker)
    def _():
        if not unrolled:
            gpad[n:] = jnp.zeros((n, rows, block), bf16)
        hpad[...] = jnp.zeros(hpad.shape, f32)
        mlag[:, n * block :] = jnp.zeros((block, block), f32)
        drain(taps_all, r_t)
        if edge:
            onward = remote(taps_all.at[:edge], taps_few, s_nt, r_nt, {"ctx": slot + n - workers})
            pl.when(far)(onward.start)
        build(taps_all, n)
        drain(gpad.at[edge:n], r_g)
        pl.semaphore_signal(mate_in, inc=1, device_id={"ch": mate})

        @apart
        def _():
            if unrolled:
                products(gpad, 1, 0)
            else:
                acc[...] = jnp.zeros(acc.shape, f32)
                over(0, n, backward_step)
            bsend[: n - edge] = acc[: (n - edge) * rows].astype(bf16).reshape(n - edge, rows, block)

        remote(bsend.at[0], bret.at[slot], s_b, r_b, {"ctx": 0}).start()
        for d in (3, 1, 2) if n == 16 else ():
            q = other(d)
            remote(bsend.at[q], bret.at[slot], s_b, r_b, {"ctx": q}).start()

        drain(vpad.at[: n - edge], r_v)

        @apart
        def _():
            over(0, lead + 1, lag_step)
            if unrolled:
                for k in range(0, lead, 2):
                    fold(k, min(2, lead - k))
            else:
                over(0, lead, fold)

        where = ch * workers + slot

        def send_lag(q, own, across):
            remote(lsend.at[q], lret.at[where], across, r_l, {"ctx": q, "ch": mate}).start()
            remote(lsend.at[q], lret.at[where], own, r_l, {"ctx": q}).start()

        pl.semaphore_wait(mate_in, 1)
        for q in range(lead):
            send_lag(q, s_l0, s_lo0)
        to_all(bsend, bret, s_b, r_b, 1, n - edge, (7, 11, 5, 9, 6, 10, 4, 8, 15, 13, 14, 12))

        @apart
        def _():
            if unrolled:
                products(vpad, 0, 1)
            else:
                acc[...] = jnp.zeros(acc.shape, f32)
                over(0, n, forward_step)
            ysend[edge:] = acc[edge * rows : total].astype(bf16).reshape(n - edge, rows, block)

        to_all(ysend, yret, s_y, r_y, edge, n)

        @apart
        def _():
            over(lead + 1, n, lag_step)
            if unrolled:
                for k in range(lead, n, 2):
                    fold(k, min(2, n - k))
            else:
                over(lead, n, fold)

        def send_lags(d, _):
            q = d + (d >= me).astype(jnp.int32)
            send_lag(q, s_l, s_lo)
            return 0

        if unrolled:
            for d in range(lead, n - 1):
                send_lags(d, 0)
        else:
            lax.fori_loop(lead, n - 1, send_lags, 0)
        pltpu.make_async_copy(lsend.at[me], lret.at[where], r_l).start()
        remote(lsend.at[me], lret.at[where], s_lo, r_l, {"ch": mate}).start()

    if edge:
        @pl.when(is_edge)
        def _():
            size = per * rows
            hpad[...] = jnp.zeros(hpad.shape, f32)
            mlag[:, edge * block : (edge + 1) * block] = jnp.zeros((block, block), f32)
            def near_products(src, shift_in, shift_out):
                for k in range(edge):
                    term = jnp.dot(
                        flat(src, k * shift_in, edge - k + k * shift_in), table(k, edge), preferred_element_type=f32
                    )
                    where = pl.ds(k * shift_out * size, (edge - k) * size)
                    if k == 0:
                        acc[where] = term
                    else:
                        acc[where] += term

            def near_forward():
                drain(taps_few, r_nt)
                build(taps_few, edge)

                @apart
                def _():
                    near_products(nv, 0, 1)
                    nysend[...] = acc[: edge * size].astype(bf16).reshape(nysend.shape)

                among(lambda p: nysend.at[p], nyret, s_y, r_ny)

            drain(nv, r_nv)
            pl.when(low)(near_forward)
            drain(nd, r_nd)

            @apart
            def _():
                for k in range(edge):
                    mlag[:, k * block : (k + 1) * block] = lax.dot_general(
                        flat(nv, 0, edge - k), flat(nd, k, edge), TN, preferred_element_type=f32
                    )
                over(0, edge, fold)

            row = (ch * 2 + high.astype(jnp.int32)) * edge + place
            for q in range(edge):
                pl.when(me != q)(remote(lsend.at[q], nlret.at[row], s_l, r_nl, {"ctx": q}).start)
                remote(lsend.at[q], nlret.at[row], s_lo, r_nl, {"ctx": q, "ch": mate}).start()

            @pl.when(low)
            def _():
                pltpu.make_async_copy(lsend.at[me], nlret.at[row], r_nl).start()

            pl.when(high)(near_forward)

            @apart
            def _():
                near_products(nd, 1, 0)
                nbsend[...] = acc[: edge * size].astype(bf16).reshape(nbsend.shape)

            among(lambda p: nbsend.at[p], nbret, s_b, r_nb)

    def put_signal(*parts):
        joined = sum(part[...].reshape(width, block).astype(f32) for part in parts)
        gs_ref[...] = joined.T.astype(bf16)

    def put_gating(*parts):
        recomputed = sum(
            lax.dot_general(flip[...], part[...].reshape(width, block), NT, preferred_element_type=f32)
            for part in parts
        )
        gg_ref[...] = (cot_ref[...].astype(f32) * recomputed).astype(bf16)

    def put_taps(*parts):
        gt_ref[...] = sum(jnp.sum(part[...], axis=0) for part in parts) * norm

    @pl.when(jnp.logical_and(me >= edge, me < n - edge))
    def _():
        drain(bret, r_b)
        put_signal(bret)
        drain(yret, r_y)
        put_gating(yret)
        drain(lret, r_l)
        put_taps(lret)

    if edge:
        @pl.when(low)
        def _():
            drain(nyret, r_ny)
            put_gating(nyret)
            drain(nbret, r_nb)
            drain(bret, r_b)
            put_signal(nbret, bret)
            drain(nlret, r_nl)
            drain(lret, r_l)
            put_taps(nlret, lret)

        @pl.when(high)
        def _():
            drain(nbret, r_nb)
            put_signal(nbret)
            drain(nyret, r_ny)
            drain(yret, r_y)
            put_gating(nyret, yret)
            drain(lret, r_l)
            put_taps(lret)

    @pl.when(is_worker)
    def _():
        drain(taps_all.at[: workers - 1], s_t)
        drain(gsend.at[: workers - 1], s_g)
        drain(vsend.at[: workers - 1], s_v)
        if edge:
            pl.when(far)(lambda: drain(taps_all.at[:edge], s_nt))
        drain(bsend.at[: n - edge - 1], s_b)
        drain(lsend.at[:lead], s_l0)
        drain(lsend.at[:lead], s_lo0)
        drain(lsend.at[: n - lead - 1], s_l)
        drain(lsend.at[: n - lead], s_lo)
        drain(ysend.at[: n - edge - 1], s_y)

    @pl.when(is_edge)
    def _():
        drain(taps_all.at[:workers], s_t)
        if edge:
            pl.when(high)(lambda: drain(gsend, s_g))
            pl.when(low)(lambda: drain(vsend, s_v))
            drain(nv.at[: edge - 1], s_nv)
            drain(nd.at[: edge - 1], s_nd)
            drain(nysend.at[: edge - 1], s_y)
            drain(nbsend.at[: edge - 1], s_b)
            pl.when(low)(lambda: drain(taps_few.at[: edge - 1], s_nt))
            pl.when(low)(lambda: drain(lsend.at[: edge - 1], s_l))
            pl.when(high)(lambda: drain(lsend.at[:edge], s_l))
            drain(lsend.at[:edge], s_lo)
        else:
            drain(gsend, s_g)
            drain(vsend, s_v)


def store(gs_in, gg_in, gt_in, gs_out, gg_out, gt_out, sems):
    copies = [
        pltpu.make_async_copy(src, dst, sems.at[i])
        for i, (src, dst) in enumerate(((gs_in, gs_out), (gg_in, gg_out), (gt_in, gt_out)))
    ]
    for copy in copies:
        copy.start()
    for copy in copies:
        copy.wait()


def body(signal, gating, filter_taps, cotangent):
    block, width = signal.shape
    n = lax.axis_size("ctx")
    pieces = lax.axis_size("ch")
    workers = WORKERS
    first = (n - workers) // 2
    rows = width // workers
    whole = n & (n - 1) == 0 and workers % 2 == 0 and first == workers // 2
    edge = first if whole else 0
    few = max(edge, 1)
    per = workers // few
    norm = 1.0 / math.sqrt(width * pieces * block * n)
    pad = 0 if n <= 16 else n
    hbm = pl.BlockSpec(memory_space=pltpu.HBM)
    vmem = pl.BlockSpec(memory_space=pltpu.VMEM)
    dma = pltpu.SemaphoreType.DMA
    results = (
        pltpu.VMEM((block, width), bf16),
        pltpu.VMEM((block, width), bf16),
        pltpu.VMEM((1, block), f32),
    )
    outputs = pl.pallas_call(
        functools.partial(kernel, n, workers, first, edge, norm),
        out_shape=results,
        in_specs=[hbm] * 4,
        out_specs=(vmem,) * 3,
        scratch_shapes=[
            pltpu.VMEM((block, width), bf16),
            pltpu.VMEM((block, width), bf16),
            pltpu.VMEM((block,), bf16),
            pltpu.VMEM((block, width), bf16),
            pltpu.VMEM((block, block), bf16),
            pltpu.VMEM((1, block), f32),
            pltpu.VMEM((workers, rows, block), bf16),
            pltpu.VMEM((workers, rows, block), bf16),
            pltpu.VMEM((n, 1, block), f32),
            pltpu.VMEM((n + pad, rows, block), bf16),
            pltpu.VMEM((n, rows, block), bf16),
            pltpu.VMEM((n, rows, block), bf16),
            pltpu.VMEM((n, rows, block), bf16),
            pltpu.VMEM((n, 1, block), f32),
            pltpu.VMEM((workers, rows, block), bf16),
            pltpu.VMEM((workers, rows, block), bf16),
            pltpu.VMEM((pieces * workers, 1, block), f32),
            pltpu.VMEM((1, (n + 1) * block + block // 2), f32),
            pltpu.VMEM((block // 2, (n + 1) * block), bf16),
            pltpu.VMEM(((n + pad) * rows, block), f32),
            pltpu.VMEM((block, (n + 1) * block), f32),
            pltpu.VMEM((few, 1, block), f32),
        ]
        + [pltpu.VMEM((few, per, rows, block), bf16)] * 6
        + [pltpu.VMEM((2 * pieces * few, 1, block), f32)]
        + [dma] * 24
        + [dma((4,)), pltpu.SemaphoreType.REGULAR, pltpu.SemaphoreType.REGULAR],
        compiler_params=pltpu.CompilerParams(
            collective_id=0, has_side_effects=True, vmem_limit_bytes=60 * 1024 * 1024
        ),
    )(signal, gating, filter_taps, cotangent)
    outputs = [pltpu.with_memory_space_constraint(o, pltpu.VMEM) for o in outputs]
    grad_signal, grad_gating, grad_taps = pl.pallas_call(
        store,
        out_shape=(
            jax.ShapeDtypeStruct((block, width), bf16),
            jax.ShapeDtypeStruct((block, width), bf16),
            jax.ShapeDtypeStruct((1, block), f32),
        ),
        in_specs=[vmem] * 3,
        out_specs=(hbm,) * 3,
        scratch_shapes=[dma((3,))],
    )(*outputs)
    return (grad_signal, grad_gating, grad_taps.reshape(block))


def solution(mesh):
    in_specs = (P("ctx", "ch"), P("ctx", "ch"), P("ctx"), P("ctx", "ch"))
    out_specs = (P("ctx", "ch"), P("ctx", "ch"), P("ctx"))
    return jax.shard_map(body, mesh=mesh, in_specs=in_specs, out_specs=out_specs, check_vma=False)
```
